32 devices in a mesh: crops: 2 (over y), rows: 4 (over x, core), cols: 4 (over z).
Axes of the slice: x: 2, y: 2, z: 4, core: 2. Of those that a mesh axis runs over, the one named last changes fastest.
Arguments:
- pair_maps: bfloat16 [2, 64, 1024, 1024], P('crops', None, 'rows', 'cols'), parts along dimension 0, may hold values from -6 to 6
- conv_a: bfloat16 [2, 3, 64, 192], replicated, may hold values from -0.25 to 0.25
- bias_a: float32 [2, 64], replicated, may hold values from -3 to 3
- conv_b: bfloat16 [2, 3, 64, 192], replicated, may hold values from -0.25 to 0.25
- bias_b: float32 [2, 64], replicated, may hold values from -3 to 3
- out_weight: bfloat16 [37, 64], replicated, may hold values from -3 to 3
- out_bias: float32 [37], replicated, may hold values from -4 to 4
Outputs:
- log_probs: float32 [2, 37, 1024, 1024], P('crops', None, ('rows', 'cols')), parts along dimension 0
The draws below stay inside these ranges and needn't reach their ends.
There are 2 independent parts, one for each index of `crops`. The reference program is written for one: setup_inputs(seed, part) draws one part's arguments, and reference() takes and returns one part's arrays. A program takes and returns all parts, laid end to end along the dimension named above; an argument that names none is the same for every part. Nothing has to cross between parts.
All inputs are finite; a program needn't handle non-finite values.
Results may differ from the reference program's by a relative error of at most 0.0045.
Values may be sent and summed in bfloat16 or wider, within the bound.
No kernel may reach another device: no remote copies, remote signals or barrier semaphores. Data moves between devices by JAX's collectives and lax.ppermute only.
A program may use at most 192 MiB of HBM per device.

```python
import jax
import jax.numpy as jnp
from jax import lax

CROPS = 1
L = 1024
C = 64
BINS = 37
BLOCKS = 2
D1 = 4
D2 = 8


def levels(stream_key, extent, split, least, largest):
    gain = 1.0
    for position, shards_of in split:
        draws = jax.random.uniform(jax.random.fold_in(jax.random.fold_in(stream_key, 6), position), (shards_of,), jnp.float32, least / len(split), largest / len(split))
        gain = gain * jnp.repeat(jnp.exp(draws), extent[position] // shards_of).reshape((-1,) + (1,) * (len(extent) - 1 - position))
    return gain


def bell_draw(stream_key, shape, spread, most, shards=(), held_as=jnp.bfloat16):
    loudness = levels(stream_key, shape, shards, -0.22, 0.18) if shards else 1.0
    drawn = jax.random.normal(stream_key, shape, jnp.float32) * spread * loudness
    return jnp.minimum(jnp.maximum(drawn, -most), most).astype(held_as)


def setup_inputs(seed: int = 0, part: int = 0) -> dict:
    seeds = jax.random.split(jax.random.key(seed), 8)
    part_splits = jax.random.split(jax.random.fold_in(seeds[7], part), 8)
    return {
        "pair_maps": bell_draw(part_splits[0], (CROPS, C, L, L), 1.0, 6.0, ((2, 4), (3, 4))),
        "conv_a": bell_draw(seeds[1], (BLOCKS, 3, C, 3 * C), (9 * C) ** -0.5, 0.25),
        "bias_a": bell_draw(seeds[2], (BLOCKS, C), 0.5, 3.0, (), jnp.float32),
        "conv_b": bell_draw(seeds[3], (BLOCKS, 3, C, 3 * C), (9 * C) ** -0.5, 0.25),
        "bias_b": bell_draw(seeds[4], (BLOCKS, C), 0.5, 3.0, (), jnp.float32),
        "out_weight": bell_draw(seeds[5], (BINS, C), 0.5, 3.0),
        "out_bias": bell_draw(seeds[6], (BINS,), 1.0, 4.0, (), jnp.float32),
    }


def convolve(image, kernel, dilation):
    height = image.shape[1]
    breadth = image.shape[2]
    padded = jnp.pad(image.astype(jnp.float32), ((0, 0), (dilation, dilation), (dilation, dilation)))
    summed = jnp.zeros((kernel.shape[1], height, breadth), jnp.float32)
    for tap_row in range(3):
        stacked = jnp.concatenate([padded[:, tap_row * dilation:tap_row * dilation + height, tap_col * dilation:tap_col * dilation + breadth] for tap_col in range(3)], axis=0)
        summed = summed + jnp.einsum("oc,chw->ohw", kernel[tap_row].astype(jnp.float32), stacked)
    return summed


def reference(pair_maps, conv_a, bias_a, conv_b, bias_b, out_weight, out_bias):
    def one_crop(image):
        field = image
        for block_index in range(BLOCKS):
            inner = jax.nn.elu(convolve(field, conv_a[block_index], D1) + bias_a[block_index][:, None, None]).astype(jnp.bfloat16)
            field = (field.astype(jnp.float32) + convolve(inner, conv_b[block_index], D2) + bias_b[block_index][:, None, None]).astype(jnp.bfloat16)
        logits = (jnp.einsum("kc,chw->khw", out_weight.astype(jnp.float32), field.astype(jnp.float32)) + out_bias[:, None, None]).astype(jnp.bfloat16)
        wide = logits.astype(jnp.float32)
        symmetric = (wide + jnp.transpose(wide, (0, 2, 1))) * 0.5
        return symmetric - jnp.log(jnp.sum(jnp.exp(symmetric), axis=0, keepdims=True))

    return lax.map(one_crop, pair_maps)
```

```python
import functools

import jax
import jax.numpy as jnp
from jax import lax
from jax.experimental import pallas as pl
from jax.experimental.pallas import tpu as pltpu
from jax.sharding import PartitionSpec as P

BLOCKS = 2
D1 = 4
D2 = 8

FAR = 1 << 20

def chain_kernel(cfg, edge_ref, xt_ref, xi_ref, xb_ref, xh_ref, wa_ref, ba_ref, wb_ref, bb_ref, wo_ref, bo_ref, o_ref, X, I, bias, acc, *xs):
    H, W, C, K, D1, D2, R, LEAD = cfg
    S = W + 64
    halo = 2 * (D1 + D2)
    NB = R * S
    BF = jnp.bfloat16
    F32 = jnp.float32
    T = 256
    def at(row):
        return pl.multiple_of(128 + (row + halo + LEAD) * S, 128)
    X[:, 64 + (LEAD * S):128 + LEAD * S] = xh_ref[0]
    def filler(ref, start):
        def fill(i, _):
            parts = []
            for r in range(R):
                parts += [ref[i * R + r], xh_ref[i * R + r + 1 + start]]
            X[:, pl.ds(at(i * R + start - halo), NB)] = jnp.concatenate(parts, axis=1)
            return 0
        return fill
    lax.fori_loop(0, halo // R, filler(xt_ref, 0), 0)
    lax.fori_loop(0, H // R, filler(xi_ref, halo), 0)
    lax.fori_loop(0, halo // R, filler(xb_ref, halo + H), 0)
    for k in range(2):
        bias[2 * k] = jnp.broadcast_to(ba_ref[k], (C, 128))
        bias[2 * k + 1] = jnp.broadcast_to(bb_ref[k], (C, 128))
    top, bottom, left, right = edge_ref[0], edge_ref[1], edge_ref[2], edge_ref[3]
    lane = lax.broadcasted_iota(jnp.int32, (8, NB), 1)
    col = lane % S
    dead = ((col >= W) & (col < W + 32) & (right > 0)) | ((col >= W + 32) & (left > 0))
    rl = jnp.where(dead, 4 * FAR, lane // S + jnp.where(col >= W + 32, 1, 0))
    first = jnp.where(top > 0, 0, -FAR)
    last = jnp.where(bottom > 0, H, FAR)

    def masked(v, row, t):
        r = rl[:, t:t + T]
        m = (r >= first - row) & (r < last - row)
        return jnp.where(m[None], v.reshape(C // 8, 8, T), 0.0).reshape(C, T)

    def biased(v, i):
        b = bias[i]
        return v + jnp.concatenate([b] * (T // 128), axis=1)

    def conv(src, d, w_ref, k, lo, hi, emit):
        n = d // R
        ring = 2 * n + 1
        total = (hi - lo) // R + 2 * n
        if total % 2:
            lo -= R
            total += 1
        def slot(j):
            return pl.multiple_of(lax.rem(j, ring) * NB, 128)
        def shift(j, xs):
            x = src[:, pl.ds(pl.multiple_of(at(lo - d + j * R) - 128, 128), NB + 256)]
            xs[0:C, :] = pltpu.roll(x, d, 1)[:, 128:128 + NB]
            xs[C:2 * C, :] = pltpu.roll(x, NB + 256 - d, 1)[:, 128:128 + NB]
        def step(j, xs, nxt):
            shift(j + 1, nxt)
            row = lo - d + j * R
            s0, s1, s2 = slot(j), slot(j + ring - n), slot(j + ring - 2 * n)
            for t in range(0, NB, T):
                x = jnp.concatenate([xs[0:C, t:t + T], src[:, pl.ds(at(row) + t, T)], xs[C:2 * C, t:t + T]], axis=0)
                y = jnp.dot(w_ref[k], x, preferred_element_type=F32)
                done = acc[:, pl.ds(s2 + t, T)] + y[2 * C:]
                acc[:, pl.ds(s1 + t, T)] += y[C:2 * C]
                acc[:, pl.ds(s0 + t, T)] = y[:C]
                emit(row - d, t, done)
        shift(0, xs[0])
        def body(i, _):
            step(2 * i, xs[0], xs[1])
            step(2 * i + 1, xs[1], xs[0])
            return 0
        lax.fori_loop(0, total // 2, body, 0)

    for k in range(2):
        edge = halo if k == 0 else D1 + D2
        def emit_a(row, t, v, k=k):
            v = biased(v, 2 * k)
            e = jnp.where(v > 0, v, jnp.exp(v) - 1.0)
            I[:, pl.ds(at(row) + t, T)] = masked(e, row, t).astype(BF)
        conv(X, D1, wa_ref, k, -(edge - D1) - R, H + edge - D1, emit_a)
        def emit_b(row, t, v, k=k):
            v = biased(v, 2 * k + 1) + X[:, pl.ds(at(row) + t, T)].astype(F32)
            if k == 0:
                v = masked(v, row, t)
            X[:, pl.ds(at(row) + t, T)] = v.astype(BF)
        lo = -(edge - D1 - D2) - (R if k == 0 else 0)
        conv(I, D2, wb_ref, k, lo, H + edge - D1 - D2, emit_b)
    bo = jnp.broadcast_to(bo_ref[...], (bo_ref.shape[0], W))
    def project(i, _):
        x = X[:, pl.ds(at(i * R), NB)]
        for r in range(R):
            g = jnp.dot(wo_ref[...], x[:, r * S:r * S + W], preferred_element_type=F32) + bo
            o_ref[i * R + r] = g.astype(BF)
        return 0
    lax.fori_loop(0, H // R, project, 0)

def chain(edge, xt, xi, xb, xh, wa, ba, wb, bb, wo, bo):
    H, C, W = xi.shape
    K = wo.shape[0]
    R = 4
    halo = 2 * (D1 + D2)
    S = W + 64
    LEAD = 2 * halo
    N = 128 + (H + 2 * halo + LEAD) * S + 256 + 2 * R * S
    KP = -(-K // 16) * 16
    wa = wa.reshape(2, 3 * C, 3 * C)
    wb = wb.reshape(2, 3 * C, 3 * C)
    wo = jnp.pad(wo, ((0, KP - K), (0, 0)))
    bo = jnp.pad(bo, (0, KP - K))[:, None]
    vm = pl.BlockSpec(memory_space=pltpu.VMEM)
    return pl.pallas_call(
        functools.partial(chain_kernel, (H, W, C, K, D1, D2, R, LEAD)),
        out_shape=jax.ShapeDtypeStruct((H, KP, W), jnp.bfloat16),
        in_specs=[pl.BlockSpec(memory_space=pltpu.SMEM)] + [vm] * 10,
        out_specs=vm,
        scratch_shapes=[pltpu.VMEM((C, N), jnp.bfloat16), pltpu.VMEM((C, N), jnp.bfloat16), pltpu.VMEM((4, C, 128), jnp.float32),
                        pltpu.VMEM((C, (2 * (max(D1, D2) // R) + 1) * R * S), jnp.float32)]
                        + [pltpu.VMEM((2 * C, R * S), jnp.bfloat16)] * 2,
        compiler_params=pltpu.CompilerParams(vmem_limit_bytes=63000 * 1024),
        name="chain",
    )(edge, xt, xi, xb, xh, wa, ba[:, :, None], wb, bb[:, :, None], wo, bo)[:, :K]


def neighbours(first, last, axis):
    peers = lax.axis_size(axis)
    up = [(i, i + 1) for i in range(peers - 1)]
    down = [(j, i) for i, j in up]
    return lax.ppermute(last, axis, up), lax.ppermute(first, axis, down)


def shards(pair_maps, conv_a, bias_a, conv_b, bias_b, out_weight, out_bias):
    halo = BLOCKS * (D1 + D2)
    rows, cols = lax.axis_size("rows"), lax.axis_size("cols")
    field = jnp.transpose(pair_maps[0], (1, 0, 2))
    above, below = neighbours(field[:halo], field[-halo:], "rows")
    west = jnp.concatenate([v[:, :, :halo] for v in (above, field, below)], axis=0)
    east = jnp.concatenate([v[:, :, -halo:] for v in (above, field, below)], axis=0)
    left, right = neighbours(west, east, "cols")
    side = jnp.concatenate(
        [
            jnp.pad(right, ((1, 0), (0, 0), (0, 64 - 2 * halo))),
            jnp.pad(left, ((0, 1), (0, 0), (0, 0))),
        ],
        axis=2,
    )
    r, c = lax.axis_index("rows"), lax.axis_index("cols")
    edge = jnp.stack([r == 0, r == rows - 1, c == 0, c == cols - 1]).astype(jnp.int32)
    logits = chain(edge, above, field, below, side, conv_a, bias_a, conv_b, bias_b, out_weight, out_bias)
    logits = jnp.transpose(logits, (1, 0, 2))[None]
    strips = lax.all_to_all(logits, "cols", split_axis=2, concat_axis=3, tiled=True)
    flipped = lax.all_to_all(strips, ("rows", "cols"), split_axis=3, concat_axis=2, tiled=True)
    mirrored = jnp.swapaxes(flipped, 2, 3)
    symmetric = (strips.astype(jnp.float32) + mirrored.astype(jnp.float32)) * 0.5
    return symmetric - jnp.log(jnp.sum(jnp.exp(symmetric), axis=1, keepdims=True))


def solution(mesh):
    in_specs = (P("crops", None, "rows", "cols"), P(), P(), P(), P(), P(), P())
    out_specs = P("crops", None, ("rows", "cols"), None)
    body = jax.shard_map(shards, mesh=mesh, in_specs=in_specs, out_specs=out_specs, check_vma=False)

    def run(*args):
        with jax.sharding.use_abstract_mesh(mesh.abstract_mesh):
            return body(*args)

    return run
```

```python
import functools

import jax
import jax.numpy as jnp
from jax import lax
from jax.experimental import pallas as pl
from jax.experimental.pallas import tpu as pltpu
from jax.sharding import PartitionSpec as P

BLOCKS = 2
D1 = 4
D2 = 8

FAR = 1 << 20

def chain_kernel(cfg, edge_ref, xt_ref, xi_ref, xb_ref, xh_ref, wa_ref, ba_ref, wb_ref, bb_ref, wo_ref, bo_ref, o_ref, X, I, bias, acc, *xs):
    H, W, C, K, D1, D2, R, LEAD = cfg
    S = W + 64
    halo = 2 * (D1 + D2)
    NB = R * S
    BF = jnp.bfloat16
    F32 = jnp.float32
    T = 256
    def at(row):
        return pl.multiple_of(128 + (row + halo + LEAD) * S, 128)
    X[:, 64 + (LEAD * S):128 + LEAD * S] = xh_ref[0]
    def filler(ref, start):
        def fill(i, _):
            parts = []
            for r in range(R):
                parts += [ref[i * R + r], xh_ref[i * R + r + 1 + start]]
            X[:, pl.ds(at(i * R + start - halo), NB)] = jnp.concatenate(parts, axis=1)
            return 0
        return fill
    lax.fori_loop(0, halo // R, filler(xt_ref, 0), 0)
    lax.fori_loop(0, H // R, filler(xi_ref, halo), 0)
    lax.fori_loop(0, halo // R, filler(xb_ref, halo + H), 0)
    for k in range(2):
        bias[2 * k] = jnp.broadcast_to(ba_ref[k], (C, 128))
        bias[2 * k + 1] = jnp.broadcast_to(bb_ref[k], (C, 128))
    top, bottom, left, right = edge_ref[0], edge_ref[1], edge_ref[2], edge_ref[3]
    lane = lax.broadcasted_iota(jnp.int32, (8, NB), 1)
    col = lane % S
    dead = ((col >= W) & (col < W + 32) & (right > 0)) | ((col >= W + 32) & (left > 0))
    rl = jnp.where(dead, 4 * FAR, lane // S + jnp.where(col >= W + 32, 1, 0))
    first = jnp.where(top > 0, 0, -FAR)
    last = jnp.where(bottom > 0, H, FAR)

    def masked(v, row, t):
        r = rl[:, t:t + T]
        m = (r >= first - row) & (r < last - row)
        return jnp.where(m[None], v.reshape(C // 8, 8, T), 0.0).reshape(C, T)

    def biased(v, i):
        b = bias[i]
        return v + jnp.concatenate([b] * (T // 128), axis=1)

    def conv(src, d, w_ref, k, lo, hi, emit):
        n = d // R
        ring = 2 * n + 1
        total = (hi - lo) // R + 2 * n
        if total % 2:
            lo -= R
            total += 1
        def slot(j):
            return pl.multiple_of(lax.rem(j, ring) * NB, 128)
        def shift(j, xs):
            x = src[:, pl.ds(pl.multiple_of(at(lo - d + j * R) - 128, 128), NB + 256)]
            xs[0:C, :] = pltpu.roll(x, d, 1)[:, 128:128 + NB]
            xs[C:2 * C, :] = pltpu.roll(x, NB + 256 - d, 1)[:, 128:128 + NB]
        def step(j, xs, nxt):
            shift(j + 1, nxt)
            row = lo - d + j * R
            s0, s1, s2 = slot(j), slot(j + ring - n), slot(j + ring - 2 * n)
            for t in range(0, NB, T):
                x = jnp.concatenate([xs[0:C, t:t + T], src[:, pl.ds(at(row) + t, T)], xs[C:2 * C, t:t + T]], axis=0)
                y = jnp.dot(w_ref[k], x, preferred_element_type=F32)
                done = acc[:, pl.ds(s2 + t, T)] + y[2 * C:]
                acc[:, pl.ds(s1 + t, T)] += y[C:2 * C]
                acc[:, pl.ds(s0 + t, T)] = y[:C]
                emit(row - d, t, done)
        shift(0, xs[0])
        def body(i, _):
            step(2 * i, xs[0], xs[1])
            step(2 * i + 1, xs[1], xs[0])
            return 0
        lax.fori_loop(0, total // 2, body, 0)

    for k in range(2):
        edge = halo if k == 0 else D1 + D2
        def emit_a(row, t, v, k=k):
            v = biased(v, 2 * k)
            e = jnp.where(v > 0, v, jnp.exp(v) - 1.0)
            I[:, pl.ds(at(row) + t, T)] = masked(e, row, t).astype(BF)
        conv(X, D1, wa_ref, k, -(edge - D1) - R, H + edge - D1, emit_a)
        def emit_b(row, t, v, k=k):
            v = biased(v, 2 * k + 1) + X[:, pl.ds(at(row) + t, T)].astype(F32)
            if k == 0:
                v = masked(v, row, t)
            X[:, pl.ds(at(row) + t, T)] = v.astype(BF)
        lo = -(edge - D1 - D2) - (R if k == 0 else 0)
        conv(I, D2, wb_ref, k, lo, H + edge - D1 - D2, emit_b)
    bo = jnp.broadcast_to(bo_ref[...], (bo_ref.shape[0], W))
    def project(i, _):
        x = X[:, pl.ds(at(i * R), NB)]
        for r in range(R):
            g = jnp.dot(wo_ref[...], x[:, r * S:r * S + W], preferred_element_type=F32) + bo
            o_ref[i * R + r] = g.astype(BF)
        return 0
    lax.fori_loop(0, H // R, project, 0)

def chain(edge, xt, xi, xb, xh, wa, ba, wb, bb, wo, bo):
    H, C, W = xi.shape
    K = wo.shape[0]
    R = 4
    halo = 2 * (D1 + D2)
    S = W + 64
    LEAD = 2 * halo
    N = 128 + (H + 2 * halo + LEAD) * S + 256 + 2 * R * S
    KP = -(-K // 16) * 16
    wa = wa.reshape(2, 3 * C, 3 * C)
    wb = wb.reshape(2, 3 * C, 3 * C)
    wo = jnp.pad(wo, ((0, KP - K), (0, 0)))
    bo = jnp.pad(bo, (0, KP - K))[:, None]
    vm = pl.BlockSpec(memory_space=pltpu.VMEM)
    return pl.pallas_call(
        functools.partial(chain_kernel, (H, W, C, K, D1, D2, R, LEAD)),
        out_shape=jax.ShapeDtypeStruct((H, KP, W), jnp.bfloat16),
        in_specs=[pl.BlockSpec(memory_space=pltpu.SMEM)] + [vm] * 10,
        out_specs=vm,
        scratch_shapes=[pltpu.VMEM((C, N), jnp.bfloat16), pltpu.VMEM((C, N), jnp.bfloat16), pltpu.VMEM((4, C, 128), jnp.float32),
                        pltpu.VMEM((C, (2 * (max(D1, D2) // R) + 1) * R * S), jnp.float32)]
                        + [pltpu.VMEM((2 * C, R * S), jnp.bfloat16)] * 2,
        compiler_params=pltpu.CompilerParams(vmem_limit_bytes=63000 * 1024),
        name="chain",
    )(edge, xt, xi, xb, xh, wa, ba[:, :, None], wb, bb[:, :, None], wo, bo)[:, :K]


def neighbours(first, last, axis):
    peers = lax.axis_size(axis)
    up = [(i, i + 1) for i in range(peers - 1)]
    down = [(j, i) for i, j in up]
    return lax.ppermute(last, axis, up), lax.ppermute(first, axis, down)


def shards(pair_maps, conv_a, bias_a, conv_b, bias_b, out_weight, out_bias):
    halo = BLOCKS * (D1 + D2)
    rows, cols = lax.axis_size("rows"), lax.axis_size("cols")
    field = jnp.transpose(pair_maps[0], (1, 0, 2))
    above, below = neighbours(field[:halo], field[-halo:], "rows")
    west = jnp.concatenate([v[:, :, :halo] for v in (above, field, below)], axis=0)
    east = jnp.concatenate([v[:, :, -halo:] for v in (above, field, below)], axis=0)
    left, right = neighbours(west, east, "cols")
    side = jnp.concatenate(
        [
            jnp.pad(right, ((1, 0), (0, 0), (0, 64 - 2 * halo))),
            jnp.pad(left, ((0, 1), (0, 0), (0, 0))),
        ],
        axis=2,
    )
    r, c = lax.axis_index("rows"), lax.axis_index("cols")
    edge = jnp.stack([r == 0, r == rows - 1, c == 0, c == cols - 1]).astype(jnp.int32)
    logits = chain(edge, above, field, below, side, conv_a, bias_a, conv_b, bias_b, out_weight, out_bias)
    if rows == 4 and cols == 4 and field.shape[0] == field.shape[2] and field.shape[0] // rows == 64:
        return square(logits)
    logits = jnp.transpose(logits, (1, 0, 2))[None]
    strips = lax.all_to_all(logits, "cols", split_axis=2, concat_axis=3, tiled=True)
    flipped = lax.all_to_all(strips, ("rows", "cols"), split_axis=3, concat_axis=2, tiled=True)
    mirrored = jnp.swapaxes(flipped, 2, 3)
    symmetric = (strips.astype(jnp.float32) + mirrored.astype(jnp.float32)) * 0.5
    return symmetric - jnp.log(jnp.sum(jnp.exp(symmetric), axis=1, keepdims=True))


def pair_kernel(r0, r1, r2, r3, lab, msg):
    K, sub, lanes = r0.shape
    for p, (one, two) in enumerate(((r0, r2), (r1, r3))):

        def add(k, total, one=one, two=two, p=p):
            v = (one[k].astype(jnp.float32) + two[k].astype(jnp.float32)) * 0.5
            lab[p, k] = v
            return total + jnp.exp(v)

        norm = jnp.log(lax.fori_loop(0, K, add, jnp.zeros((sub, lanes), jnp.float32)))

        def emit(k, carry, p=p, norm=norm):
            v = lab[p, k] - norm
            lab[p, k] = v
            w = v.T
            for t in range(lanes // sub):
                b = w[t * sub:(t + 1) * sub]
                msg[p, t, k] = jnp.concatenate([b[:sub // 2], b[sub // 2:]], axis=1).astype(jnp.bfloat16)
            return carry

        lax.fori_loop(0, K, emit, 0)


def pairs(recs):
    K, sub, W = recs[0].shape
    lanes = 128
    return pl.pallas_call(
        pair_kernel,
        grid=(W // lanes,),
        in_specs=[pl.BlockSpec((K, sub, lanes), lambda i: (0, 0, i))] * 4,
        out_specs=[
            pl.BlockSpec((2, K, sub, lanes), lambda i: (0, 0, 0, i)),
            pl.BlockSpec((2, lanes // sub, K, sub // 2, 2 * sub), lambda i: (0, i, 0, 0, 0)),
        ],
        out_shape=[
            jax.ShapeDtypeStruct((2, K, sub, W), jnp.float32),
            jax.ShapeDtypeStruct((2, W // sub, K, sub // 2, 2 * sub), jnp.bfloat16),
        ],
        name="pairs",
    )(*recs)


def own_kernel(a_ref, b_ref, o_ref, tmp):
    K = a_ref.shape[0]

    def add(k, total):
        v = (a_ref[k].astype(jnp.float32) + b_ref[k].astype(jnp.float32)) * 0.5
        tmp[k] = v
        return total + jnp.exp(v)

    norm = jnp.log(lax.fori_loop(0, K, add, jnp.zeros(tmp.shape[1:], jnp.float32)))

    def emit(k, carry):
        o_ref[k] = (tmp[k] - norm).astype(jnp.bfloat16)
        return carry

    lax.fori_loop(0, K, emit, 0)


def own_pairs(tile, turned):
    K, H, W = tile.shape
    step = 32
    spec = pl.BlockSpec((K, step, W), lambda i: (0, i, 0))
    return pl.pallas_call(
        own_kernel,
        grid=(H // step,),
        in_specs=[spec, spec],
        out_specs=spec,
        out_shape=jax.ShapeDtypeStruct((K, H, W), jnp.bfloat16),
        scratch_shapes=[pltpu.VMEM((K, step, W), jnp.float32)],
        cost_estimate=pl.CostEstimate(flops=6 * K * H * W, bytes_accessed=6 * K * H * W, transcendentals=K * H * W),
        name="own",
    )(tile, turned)


def place_kernel(n, where_ref, diag, lab, *refs):
    o_ref = refs[-1]
    near, far = refs[:n], refs[n:2 * n]
    K, sub, W = diag.shape
    r, s = where_ref[0], where_ref[1]
    keeps = where_ref[2]

    def column(tile):
        return pl.multiple_of(lax.rem(tile, n) * W, W)

    def unpacked(source, k):
        parts = []
        for b in source:
            v = b[k].astype(jnp.float32)
            parts.append(jnp.concatenate([v[:, :sub], v[:, sub:]], axis=0))
        return parts

    def spread(source, k, tile):
        got = unpacked(source, k)
        for q in range(0, n, 2):
            pieces = []
            for b in (q, q + 1):
                v = got[0]
                for shift in range(1, n):
                    v = jnp.where(lax.rem(s + n - b, n) == shift, got[shift], v)
                pieces.append(v)
            o_ref[k, :, pl.ds(pl.multiple_of(column(tile) + q * sub, 2 * sub), 2 * sub)] = jnp.concatenate(pieces, axis=1)

    def body(k, carry):
        o_ref[k, :, pl.ds(column(r), W)] = diag[k].astype(jnp.float32)
        o_ref[k, :, pl.ds(column(r + 1), W)] = lab[lax.rem(s, 2), k]
        spread(near, k, r + n - 1)

        @pl.when(keeps > 0)
        def _():
            o_ref[k, :, pl.ds(column(r + 2), W)] = lab[1 - lax.rem(s, 2), k]

        @pl.when(keeps == 0)
        def _():
            spread(far, k, r + 2)

        return carry

    lax.fori_loop(0, K, body, 0)


def place(where, diag, lab, near, far):
    K, sub, W = diag.shape
    n = len(near)
    vm = pl.BlockSpec(memory_space=pltpu.VMEM)
    return pl.pallas_call(
        functools.partial(place_kernel, n),
        in_specs=[pl.BlockSpec(memory_space=pltpu.SMEM)] + [vm] * (2 + 2 * n),
        out_specs=vm,
        out_shape=jax.ShapeDtypeStruct((K, sub, n * W), jnp.float32),
        compiler_params=pltpu.CompilerParams(vmem_limit_bytes=40 * 1024 * 1024),
        name="place",
    )(where, diag, lab, *near, *far)


def plan(n):
    homes = {}
    for r in range(n):
        for c in range(n):
            gap = (c - r) % n
            if gap == 1:
                homes[r, c] = (r, 0, 0)
            elif gap == 3:
                homes[r, c] = (c, 1, 2)
            elif gap == 2:
                owner = 0 if 0 in (r, c) else 3
                homes[r, c] = (owner, int(r != owner), 1 if r == owner else 3)
    return homes


def square(logits):
    n = lax.axis_size("rows")
    axes = ("rows", "cols")
    r, s = lax.axis_index("rows"), lax.axis_index("cols")
    me = r * n + s
    H, K, W = logits.shape
    sub = H // n
    homes = plan(n)
    turn = jnp.array([homes.get((i // n, i % n), (0, 0, 0))[1] for i in range(n * n)])[me]
    off = jnp.array([homes.get((i // n, i % n), (0, 0, 0))[2] for i in range(n * n)])[me]
    tile = jnp.transpose(logits, (1, 0, 2))
    turned = jnp.swapaxes(tile, 1, 2)
    recs = []
    for m in range(n):
        start = lax.rem(off + m, n) * sub
        a = lax.dynamic_slice_in_dim(tile, start, sub, 1)
        b = lax.dynamic_slice_in_dim(turned, start, sub, 1)
        perm = [(i * n + j, home * n + (m + o) % n) for (i, j), (home, _, o) in homes.items()]
        recs.append(lax.ppermute(jnp.where(turn > 0, b, a), axes, perm))
    own = own_pairs(tile, turned)
    diag = None
    for k in range(n):
        strip = lax.dynamic_slice_in_dim(own, lax.rem(r + k, n) * sub, sub, 1)
        if k == 0:
            diag = jnp.where(s == r, strip, jnp.zeros_like(strip))
        else:
            diag = diag + lax.ppermute(strip, axes, [(i * n + i, i * n + (i + k) % n) for i in range(n)])
    lab, msg = pairs(recs)
    near, far = [], []
    for k in range(n):
        t = lax.rem(s + k, n)
        for half, kept, moves in ((lax.rem(s, 2), near, [(i, (i + 1) % n) for i in range(n)]), (1 - lax.rem(s, 2), far, [(0, 2), (3, 1)])):
            payload = lax.dynamic_slice(msg, (half, t, 0, 0, 0), (1, 1) + msg.shape[2:])[0, 0]
            perm = [(i * n + j, o * n + (j + k) % n) for i, o in moves for j in range(n)]
            kept.append(lax.ppermute(payload, axes, perm))
    keeps = jnp.where((r == 0) | (r == n - 1), 1, 0)
    where = jnp.stack([r, s, keeps]).astype(jnp.int32)
    return place(where, diag, lab, near, far)[None]


def solution(mesh):
    in_specs = (P("crops", None, "rows", "cols"), P(), P(), P(), P(), P(), P())
    out_specs = P("crops", None, ("rows", "cols"), None)
    body = jax.shard_map(shards, mesh=mesh, in_specs=in_specs, out_specs=out_specs, check_vma=False)

    def run(*args):
        with jax.sharding.use_abstract_mesh(mesh.abstract_mesh):
            return body(*args)

    return run
```

```python
import functools

import jax
import jax.numpy as jnp
from jax import lax
from jax.experimental import pallas as pl
from jax.experimental.pallas import tpu as pltpu
from jax.sharding import PartitionSpec as P

BLOCKS = 2
D1 = 4
D2 = 8
CHUNKS = 1

FAR = 1 << 20
ROWS = 4
LEAD = 16


def chain_kernel(cfg, info_ref, f_ref, wa_ref, ba_ref, wb_ref, bb_ref, wo_ref, bo_ref, o_ref, buf, sem, X, I, bias, acc, xa, xb):
    H, W, C, whole = cfg
    R = ROWS
    S = f_ref.shape[2]
    halo = BLOCKS * (D1 + D2)
    NB = R * S
    T = 256
    BF, F32 = jnp.bfloat16, jnp.float32
    start = info_ref[4]
    copy = pltpu.make_async_copy(f_ref.at[pl.ds(start, H + 2 * halo)], buf, sem)
    copy.start()

    def at(row):
        return pl.multiple_of(128 + (row + halo + LEAD) * S, 128)

    for k in range(BLOCKS):
        bias[2 * k] = jnp.broadcast_to(ba_ref[k], (C, 128))
        bias[2 * k + 1] = jnp.broadcast_to(bb_ref[k], (C, 128))
    copy.wait()

    def fill(i, _):
        X[:, pl.ds(at(i * R - halo), NB)] = jnp.concatenate([buf[i * R + q] for q in range(R)], axis=1)
        return 0

    lax.fori_loop(0, (H + 2 * halo) // R, fill, 0)
    lane = lax.broadcasted_iota(jnp.int32, (8, NB), 1)
    col = lane % S
    dead = ((col < halo) & (info_ref[2] > 0)) | ((col >= halo + W) & (info_ref[3] > 0))
    rl = jnp.where(dead, 4 * FAR, lane // S)
    first = jnp.where(info_ref[0] > 0, -start, -FAR)
    last = jnp.where(info_ref[1] > 0, whole - start, FAR)

    def masked(v, row, t):
        p = rl[:, t:t + T]
        m = (p >= first - row) & (p < last - row)
        return jnp.where(m[None], v.reshape(C // 8, 8, T), 0.0).reshape(C, T)

    def biased(v, i):
        b = bias[i]
        return v + jnp.concatenate([b] * (T // 128), axis=1)

    def conv(src, d, w_ref, k, lo, hi, emit):
        n = d // R
        ring = 2 * n + 1
        total = (hi - lo) // R + 2 * n
        if total % 2:
            lo -= R
            total += 1

        def slot(j):
            return pl.multiple_of(lax.rem(j, ring) * NB, 128)

        def shift(j, xs):
            x = src[:, pl.ds(pl.multiple_of(at(lo - d + j * R) - 128, 128), NB + 256)]
            xs[0:C, :] = pltpu.roll(x, d, 1)[:, 128:128 + NB]
            xs[C:2 * C, :] = pltpu.roll(x, NB + 256 - d, 1)[:, 128:128 + NB]

        def step(j, xs, nxt):
            shift(j + 1, nxt)
            row = lo - d + j * R
            s0, s1, s2 = slot(j), slot(j + ring - n), slot(j + ring - 2 * n)
            for t in range(0, NB, T):
                x = jnp.concatenate([xs[0:C, t:t + T], src[:, pl.ds(at(row) + t, T)], xs[C:2 * C, t:t + T]], axis=0)
                y = jnp.dot(w_ref[k], x, preferred_element_type=F32)
                done = acc[:, pl.ds(s2 + t, T)] + y[2 * C:]
                acc[:, pl.ds(s1 + t, T)] += y[C:2 * C]
                acc[:, pl.ds(s0 + t, T)] = y[:C]
                emit(row - d, t, done)

        shift(0, xa)

        def body(i, _):
            step(2 * i, xa, xb)
            step(2 * i + 1, xb, xa)
            return 0

        lax.fori_loop(0, total // 2, body, 0)

    for k in range(BLOCKS):
        edge = (BLOCKS - k) * (D1 + D2)

        def emit_a(row, t, v, k=k):
            v = biased(v, 2 * k)
            e = jnp.where(v > 0, v, jnp.exp(v) - 1.0)
            I[:, pl.ds(at(row) + t, T)] = masked(e, row, t).astype(BF)

        conv(X, D1, wa_ref, k, -(edge - D1), H + edge - D1, emit_a)

        def emit_b(row, t, v, k=k):
            v = biased(v, 2 * k + 1) + X[:, pl.ds(at(row) + t, T)].astype(F32)
            if k < BLOCKS - 1:
                v = masked(v, row, t)
            X[:, pl.ds(at(row) + t, T)] = v.astype(BF)

        conv(I, D2, wb_ref, k, -(edge - D1 - D2), H + edge - D1 - D2, emit_b)
    bo = jnp.broadcast_to(bo_ref[...], (bo_ref.shape[0], W))

    def project(i, _):
        x = X[:, pl.ds(at(i * R), NB)]
        for q in range(R):
            g = jnp.dot(wo_ref[...], x[:, q * S + halo:q * S + halo + W], preferred_element_type=F32) + bo
            o_ref[i * R + q] = g.astype(BF)
        return 0

    lax.fori_loop(0, H // R, project, 0)


def chain(info, field, wa, ba, wb, bb, wo, bo, H, W, whole):
    _, C, S = field.shape
    K = wo.shape[0]
    R = ROWS
    halo = BLOCKS * (D1 + D2)
    N = 128 + (H + 2 * halo + LEAD + R) * S + 256
    KP = -(-K // 16) * 16
    wo = jnp.pad(wo, ((0, KP - K), (0, 0)))
    bo = jnp.pad(bo, (0, KP - K))[:, None]
    vm = pl.BlockSpec(memory_space=pltpu.VMEM)
    ring = (2 * (max(D1, D2) // R) + 1) * R * S
    flops = 2 * BLOCKS * 2 * 9 * C * C * H * S
    out = pl.pallas_call(
        functools.partial(chain_kernel, (H, W, C, whole)),
        out_shape=jax.ShapeDtypeStruct((H, KP, W), jnp.bfloat16),
        in_specs=[pl.BlockSpec(memory_space=pltpu.SMEM), pl.BlockSpec(memory_space=pltpu.HBM)] + [vm] * 6,
        out_specs=vm,
        scratch_shapes=[
            pltpu.VMEM((H + 2 * halo, C, S), jnp.bfloat16),
            pltpu.SemaphoreType.DMA,
            pltpu.VMEM((C, N), jnp.bfloat16),
            pltpu.VMEM((C, N), jnp.bfloat16),
            pltpu.VMEM((2 * BLOCKS, C, 128), jnp.float32),
            pltpu.VMEM((C, ring), jnp.float32),
            pltpu.VMEM((2 * C, R * S), jnp.bfloat16),
            pltpu.VMEM((2 * C, R * S), jnp.bfloat16),
        ],
        compiler_params=pltpu.CompilerParams(vmem_limit_bytes=63000 * 1024),
        cost_estimate=pl.CostEstimate(flops=flops, bytes_accessed=4 * C * H * S, transcendentals=2 * C * H * S),
        name="chain",
    )(info, field, wa, ba[:, :, None], wb, bb[:, :, None], wo, bo)
    return out[:, :K]


def neighbours(first, last, axis):
    peers = lax.axis_size(axis)
    up = [(i, i + 1) for i in range(peers - 1)]
    down = [(j, i) for i, j in up]
    return lax.ppermute(last, axis, up), lax.ppermute(first, axis, down)


def widened(tile):
    halo = BLOCKS * (D1 + D2)
    C = tile.shape[0]
    above, below = neighbours(tile[:, :halo], tile[:, -halo:], "rows")
    left, right = neighbours(tile[:, :, :halo], tile[:, :, -halo:], "cols")
    ends = jnp.concatenate([left[:, :halo], right[:, :halo]], axis=2), jnp.concatenate([left[:, -halo:], right[:, -halo:]], axis=2)
    up, down = neighbours(*ends, "rows")
    fill = 64 - 2 * halo
    rows = []
    for west, middle, east in ((up[:, :, :halo], above, up[:, :, halo:]), (left, tile, right), (down[:, :, :halo], below, down[:, :, halo:])):
        gap = jnp.zeros((C, middle.shape[1], fill), tile.dtype)
        rows.append(jnp.concatenate([west, middle, east, gap], axis=2))
    rows.append(jnp.zeros((C, fill, rows[0].shape[2]), tile.dtype))
    return jnp.concatenate(rows, axis=1)


def shards(pair_maps, conv_a, bias_a, conv_b, bias_b, out_weight, out_bias):
    rows, cols = lax.axis_size("rows"), lax.axis_size("cols")
    _, C, H, W = pair_maps.shape
    r, c = lax.axis_index("rows"), lax.axis_index("cols")
    edge = jnp.stack([r == 0, r == rows - 1, c == 0, c == cols - 1]).astype(jnp.int32)
    field = widened(pair_maps[0])
    square_grid = rows == 4 and cols == 4 and H == W and H // rows == 64

    def call(info, field, wa, wb, length):
        return chain(info, field, wa, bias_a, wb, bias_b, out_weight, out_bias, length, W, H)

    def merged(w):
        return w.reshape(BLOCKS, 3 * C, 3 * C)

    if square_grid:
        me = r * cols + c
        homes = plan(cols)
        turn, off = (jnp.array([homes.get((i // cols, i % cols), (0, 0, 0))[q] for i in range(rows * cols)])[me] for q in (1, 2))
        field = lax.cond(turn > 0, lambda v: jnp.transpose(v, (2, 0, 1)), lambda v: jnp.transpose(v, (1, 0, 2)), field)
        edge = jnp.where(turn > 0, edge[jnp.array([2, 3, 0, 1])], edge)

        def turned(w):
            other = jnp.transpose(w.reshape(BLOCKS, 3, C, 3, C), (0, 3, 2, 1, 4))
            return jnp.where(turn > 0, merged(other), merged(w))

        wa, wb = turned(conv_a), turned(conv_b)
        q = cols // CHUNKS
        chunks = []
        for j in range(CHUNKS):
            start = ((j * q) ^ (off & ~(q - 1))) * (H // cols)
            chunks.append(jnp.transpose(call(jnp.append(edge, start), field, wa, wb, H // CHUNKS), (1, 0, 2)))
        return square(chunks, homes, off)
    field = jnp.transpose(field, (1, 0, 2))
    logits = call(jnp.append(edge, 0), field, merged(conv_a), merged(conv_b), H)
    logits = jnp.transpose(logits, (1, 0, 2))[None]
    strips = lax.all_to_all(logits, "cols", split_axis=2, concat_axis=3, tiled=True)
    flipped = lax.all_to_all(strips, ("rows", "cols"), split_axis=3, concat_axis=2, tiled=True)
    mirrored = jnp.swapaxes(flipped, 2, 3)
    symmetric = (strips.astype(jnp.float32) + mirrored.astype(jnp.float32)) * 0.5
    return symmetric - jnp.log(jnp.sum(jnp.exp(symmetric), axis=1, keepdims=True))


def pair_kernel(r0, r1, r2, r3, lab, msg):
    K, sub, lanes = r0.shape
    for p, (one, two) in enumerate(((r0, r2), (r1, r3))):

        def add(k, total, one=one, two=two, p=p):
            v = (one[k].astype(jnp.float32) + two[k].astype(jnp.float32)) * 0.5
            lab[p, k] = v
            return total + jnp.exp(v)

        norm = jnp.log(lax.fori_loop(0, K, add, jnp.zeros((sub, lanes), jnp.float32), unroll=True))

        def emit(k, carry, p=p, norm=norm):
            v = lab[p, k] - norm
            lab[p, k] = v
            w = v.T
            for t in range(lanes // sub):
                b = w[t * sub:(t + 1) * sub]
                msg[p, t, k] = jnp.concatenate([b[:sub // 2], b[sub // 2:]], axis=1).astype(jnp.bfloat16)
            return carry

        lax.fori_loop(0, K, emit, 0, unroll=True)


def pairs(recs):
    K, sub, W = recs[0].shape
    lanes = 128
    return pl.pallas_call(
        pair_kernel,
        grid=(W // lanes,),
        in_specs=[pl.BlockSpec((K, sub, lanes), lambda i: (0, 0, i))] * 4,
        out_specs=[
            pl.BlockSpec((2, K, sub, lanes), lambda i: (0, 0, 0, i)),
            pl.BlockSpec((2, lanes // sub, K, sub // 2, 2 * sub), lambda i: (0, i, 0, 0, 0)),
        ],
        out_shape=[
            jax.ShapeDtypeStruct((2, K, sub, W), jnp.float32),
            jax.ShapeDtypeStruct((2, W // sub, K, sub // 2, 2 * sub), jnp.bfloat16),
        ],
        name="pairs",
    )(*recs)


def own_kernel(a_ref, b_ref, o_ref, tmp):
    K = a_ref.shape[0]

    def add(k, total):
        v = (a_ref[k].astype(jnp.float32) + b_ref[k].astype(jnp.float32).T) * 0.5
        tmp[k] = v
        return total + jnp.exp(v)

    norm = jnp.log(lax.fori_loop(0, K, add, jnp.zeros(tmp.shape[1:], jnp.float32)))

    def emit(k, carry):
        o_ref[k] = (tmp[k] - norm).astype(jnp.bfloat16)
        return carry

    lax.fori_loop(0, K, emit, 0)


def own_pairs(tile):
    K, H, W = tile.shape
    B = 128
    return pl.pallas_call(
        own_kernel,
        grid=(H // B, W // B),
        in_specs=[pl.BlockSpec((K, B, B), lambda i, j: (0, i, j)), pl.BlockSpec((K, B, B), lambda i, j: (0, j, i))],
        out_specs=pl.BlockSpec((K, B, B), lambda i, j: (0, i, j)),
        out_shape=jax.ShapeDtypeStruct((K, H, W), jnp.bfloat16),
        scratch_shapes=[pltpu.VMEM((K, B, B), jnp.float32)],
        cost_estimate=pl.CostEstimate(flops=6 * K * H * W, bytes_accessed=6 * K * H * W, transcendentals=K * H * W),
        name="own",
    )(tile, tile)


def place_kernel(n, where_ref, diag, lab, *refs):
    o_ref = refs[-1]
    near, far = refs[:n], refs[n:2 * n]
    K, sub, W = diag.shape
    r, s = where_ref[0], where_ref[1]
    keeps = where_ref[2]

    def column(tile):
        return pl.multiple_of(lax.rem(tile, n) * W, W)

    def unpacked(source, k):
        parts = []
        for b in source:
            v = b[k].astype(jnp.float32)
            parts.append(jnp.concatenate([v[:, :sub], v[:, sub:]], axis=0))
        return parts

    def spread(source, k, tile):
        got = unpacked(source, k)
        for q in range(0, n, 2):
            pieces = []
            for b in (q, q + 1):
                v = got[0]
                for shift in range(1, n):
                    v = jnp.where(lax.rem(s + n - b, n) == shift, got[shift], v)
                pieces.append(v)
            o_ref[k, :, pl.ds(pl.multiple_of(column(tile) + q * sub, 2 * sub), 2 * sub)] = jnp.concatenate(pieces, axis=1)

    def body(k, carry):
        o_ref[k, :, pl.ds(column(r), W)] = diag[k].astype(jnp.float32)
        o_ref[k, :, pl.ds(column(r + 1), W)] = lab[lax.rem(s, 2), k]
        spread(near, k, r + n - 1)

        @pl.when(keeps > 0)
        def _():
            o_ref[k, :, pl.ds(column(r + 2), W)] = lab[1 - lax.rem(s, 2), k]

        @pl.when(keeps == 0)
        def _():
            spread(far, k, r + 2)

        return carry

    lax.fori_loop(0, K, body, 0)


def place(where, diag, lab, near, far):
    K, sub, W = diag.shape
    n = len(near)
    vm = pl.BlockSpec(memory_space=pltpu.VMEM)
    return pl.pallas_call(
        functools.partial(place_kernel, n),
        in_specs=[pl.BlockSpec(memory_space=pltpu.SMEM)] + [vm] * (2 + 2 * n),
        out_specs=vm,
        out_shape=jax.ShapeDtypeStruct((K, sub, n * W), jnp.float32),
        compiler_params=pltpu.CompilerParams(vmem_limit_bytes=40 * 1024 * 1024),
        name="place",
    )(where, diag, lab, *near, *far)


def plan(n):
    homes = {}
    for r in range(n):
        for c in range(n):
            gap = (c - r) % n
            if gap == 1:
                homes[r, c] = (r, 0, 0)
            elif gap == 3:
                homes[r, c] = (c, 1, 2)
            elif gap == 2:
                owner = 0 if 0 in (r, c) else 3
                homes[r, c] = (owner, int(r != owner), 1 if r == owner else 3)
    return homes


def square(chunks, homes, off):
    n = lax.axis_size("rows")
    axes = ("rows", "cols")
    r, s = lax.axis_index("rows"), lax.axis_index("cols")
    q = n // len(chunks)
    sub = chunks[0].shape[1] // q
    recs = []
    for m in range(n):
        strip = chunks[m // q]
        if q > 1:
            strip = lax.dynamic_slice_in_dim(strip, ((m % q) ^ (off & (q - 1))) * sub, sub, 1)
        perm = [(i * n + j, home * n + (m ^ o)) for (i, j), (home, _, o) in homes.items()]
        recs.append(lax.ppermute(strip, axes, perm))
    own = own_pairs(jnp.concatenate(chunks, axis=1))
    diag = None
    for k in range(n):
        strip = lax.dynamic_slice_in_dim(own, lax.rem(r + k, n) * sub, sub, 1)
        if k == 0:
            diag = jnp.where(s == r, strip, jnp.zeros_like(strip))
        else:
            diag = diag + lax.ppermute(strip, axes, [(i * n + i, i * n + (i + k) % n) for i in range(n)])
    lab, msg = pairs(recs)
    near, far = [], []
    for k in range(n):
        t = lax.rem(s + k, n)
        for half, kept, moves in ((lax.rem(s, 2), near, [(i, (i + 1) % n) for i in range(n)]), (1 - lax.rem(s, 2), far, [(0, 2), (3, 1)])):
            payload = lax.dynamic_slice(msg, (half, t, 0, 0, 0), (1, 1) + msg.shape[2:])[0, 0]
            perm = [(i * n + j, o * n + (j + k) % n) for i, o in moves for j in range(n)]
            kept.append(lax.ppermute(payload, axes, perm))
    keeps = jnp.where((r == 0) | (r == n - 1), 1, 0)
    where = jnp.stack([r, s, keeps]).astype(jnp.int32)
    return place(where, diag, lab, near, far)[None]


def solution(mesh):
    in_specs = (P("crops", None, "rows", "cols"), P(), P(), P(), P(), P(), P())
    out_specs = P("crops", None, ("rows", "cols"), None)
    body = jax.shard_map(shards, mesh=mesh, in_specs=in_specs, out_specs=out_specs, check_vma=False)

    def run(*args):
        with jax.sharding.use_abstract_mesh(mesh.abstract_mesh):
            return body(*args)

    return run
```

```python
import functools

import jax
import jax.numpy as jnp
from jax import lax
from jax.experimental import pallas as pl
from jax.experimental.pallas import tpu as pltpu
from jax.sharding import PartitionSpec as P

BLOCKS = 2
D1 = 4
D2 = 8
CHUNKS = 2

FAR = 1 << 20
ROWS = 4
LEAD = 16


def chain_kernel(cfg, info_ref, t_ref, f_ref, b_ref, e_ref, wa_ref, ba_ref, wb_ref, bb_ref, wo_ref, bo_ref, o_ref, buf, side, sems, X, I, bias, acc, xa, xb):
    H, W, C, whole = cfg
    R = ROWS
    S = W + e_ref.shape[2]
    halo = BLOCKS * (D1 + D2)
    NB = R * S
    T = 256
    BF, F32 = jnp.bfloat16, jnp.float32
    start = info_ref[4]
    def moved(source, a, b, length, q):
        return pltpu.make_async_copy(source.at[pl.ds(a, length)], buf.at[pl.ds(b, length)], sems.at[q])

    middle = moved(f_ref, start, halo, H, 0)
    middle.start()
    sides = pltpu.make_async_copy(e_ref.at[pl.ds(start, H + 2 * halo)], side, sems.at[3])
    sides.start()
    for q, edge_ref, outer, a, b in ((1, t_ref, start == 0, start - halo, 0), (2, b_ref, start + H == whole, start + H, H + halo)):

        @pl.when(outer)
        def _(q=q, edge_ref=edge_ref, b=b):
            moved(edge_ref, 0, b, halo, q).start()

        @pl.when(jnp.logical_not(outer))
        def _(q=q, a=a, b=b):
            moved(f_ref, a, b, halo, q).start()

    def at(row):
        return pl.multiple_of(128 + (row + halo + LEAD) * S, 128)

    for k in range(BLOCKS):
        bias[2 * k] = jnp.broadcast_to(ba_ref[k], (C, 128))
        bias[2 * k + 1] = jnp.broadcast_to(bb_ref[k], (C, 128))
    middle.wait()
    sides.wait()
    moved(t_ref, 0, 0, halo, 1).wait()
    moved(b_ref, 0, H + halo, halo, 2).wait()

    def fill(i, _):
        parts = []
        for q in range(R):
            e = side[i * R + q]
            parts += [e[:, :halo], buf[i * R + q], e[:, halo:]]
        X[:, pl.ds(at(i * R - halo), NB)] = jnp.concatenate(parts, axis=1)
        return 0

    lax.fori_loop(0, (H + 2 * halo) // R, fill, 0)
    lane = lax.broadcasted_iota(jnp.int32, (8, NB), 1)
    col = lane % S
    dead = ((col < halo) & (info_ref[2] > 0)) | ((col >= halo + W) & (info_ref[3] > 0))
    rl = jnp.where(dead, 4 * FAR, lane // S)
    first = jnp.where(info_ref[0] > 0, -start, -FAR)
    last = jnp.where(info_ref[1] > 0, whole - start, FAR)

    def masked(v, row, t):
        p = rl[:, t:t + T]
        m = (p >= first - row) & (p < last - row)
        return jnp.where(m[None], v.reshape(C // 8, 8, T), 0.0).reshape(C, T)

    def biased(v, i):
        b = bias[i]
        return v + jnp.concatenate([b] * (T // 128), axis=1)

    def conv(src, d, w_ref, k, lo, hi, emit):
        n = d // R
        ring = 2 * n + 1
        total = (hi - lo) // R + 2 * n
        if total % 2:
            lo -= R
            total += 1

        def slot(j):
            return pl.multiple_of(lax.rem(j, ring) * NB, 128)

        def shift(j, xs):
            x = src[:, pl.ds(pl.multiple_of(at(lo - d + j * R) - 128, 128), NB + 256)]
            xs[0:C, :] = pltpu.roll(x, d, 1)[:, 128:128 + NB]
            xs[C:2 * C, :] = pltpu.roll(x, NB + 256 - d, 1)[:, 128:128 + NB]

        def step(j, xs, nxt):
            shift(j + 1, nxt)
            row = lo - d + j * R
            s0, s1, s2 = slot(j), slot(j + ring - n), slot(j + ring - 2 * n)
            for t in range(0, NB, T):
                x = jnp.concatenate([xs[0:C, t:t + T], src[:, pl.ds(at(row) + t, T)], xs[C:2 * C, t:t + T]], axis=0)
                y = jnp.dot(w_ref[k], x, preferred_element_type=F32)
                done = acc[:, pl.ds(s2 + t, T)] + y[2 * C:]
                acc[:, pl.ds(s1 + t, T)] += y[C:2 * C]
                acc[:, pl.ds(s0 + t, T)] = y[:C]
                emit(row - d, t, done)

        shift(0, xa)

        def body(i, _):
            step(2 * i, xa, xb)
            step(2 * i + 1, xb, xa)
            return 0

        lax.fori_loop(0, total // 2, body, 0)

    for k in range(BLOCKS):
        edge = (BLOCKS - k) * (D1 + D2)

        def emit_a(row, t, v, k=k):
            v = biased(v, 2 * k)
            e = jnp.where(v > 0, v, jnp.exp(v) - 1.0)
            I[:, pl.ds(at(row) + t, T)] = masked(e, row, t).astype(BF)

        conv(X, D1, wa_ref, k, -(edge - D1), H + edge - D1, emit_a)

        def emit_b(row, t, v, k=k):
            v = biased(v, 2 * k + 1) + X[:, pl.ds(at(row) + t, T)].astype(F32)
            if k < BLOCKS - 1:
                v = masked(v, row, t)
            X[:, pl.ds(at(row) + t, T)] = v.astype(BF)

        conv(I, D2, wb_ref, k, -(edge - D1 - D2), H + edge - D1 - D2, emit_b)
    bo = jnp.broadcast_to(bo_ref[...], (bo_ref.shape[0], W))

    def project(i, _):
        x = X[:, pl.ds(at(i * R), NB)]
        for q in range(R):
            g = jnp.dot(wo_ref[...], x[:, q * S + halo:q * S + halo + W], preferred_element_type=F32) + bo
            o_ref[i * R + q] = g.astype(BF)
        return 0

    lax.fori_loop(0, H // R, project, 0)


def chain(info, top, field, bottom, side, wa, ba, wb, bb, wo, bo, H):
    whole, C, W = field.shape
    S = W + side.shape[2]
    K = wo.shape[0]
    R = ROWS
    halo = BLOCKS * (D1 + D2)
    N = 128 + (H + 2 * halo + LEAD + R) * S + 256
    KP = -(-K // 16) * 16
    wo = jnp.pad(wo, ((0, KP - K), (0, 0)))
    bo = jnp.pad(bo, (0, KP - K))[:, None]
    vm = pl.BlockSpec(memory_space=pltpu.VMEM)
    ring = (2 * (max(D1, D2) // R) + 1) * R * S
    flops = 2 * BLOCKS * 2 * 9 * C * C * H * S
    out = pl.pallas_call(
        functools.partial(chain_kernel, (H, W, C, whole)),
        out_shape=jax.ShapeDtypeStruct((H, KP, W), jnp.bfloat16),
        in_specs=[pl.BlockSpec(memory_space=pltpu.SMEM), *[pl.BlockSpec(memory_space=pltpu.HBM)] * 4] + [vm] * 6,
        out_specs=vm,
        scratch_shapes=[
            pltpu.VMEM((H + 2 * halo, C, W), jnp.bfloat16),
            pltpu.VMEM((H + 2 * halo, C, S - W), jnp.bfloat16),
            pltpu.SemaphoreType.DMA((4,)),
            pltpu.VMEM((C, N), jnp.bfloat16),
            pltpu.VMEM((C, N), jnp.bfloat16),
            pltpu.VMEM((2 * BLOCKS, C, 128), jnp.float32),
            pltpu.VMEM((C, ring), jnp.float32),
            pltpu.VMEM((2 * C, R * S), jnp.bfloat16),
            pltpu.VMEM((2 * C, R * S), jnp.bfloat16),
        ],
        compiler_params=pltpu.CompilerParams(vmem_limit_bytes=63000 * 1024),
        cost_estimate=pl.CostEstimate(flops=flops, bytes_accessed=4 * C * H * S, transcendentals=2 * C * H * S),
        name="chain",
    )(info, top, field, bottom, side, wa, ba[:, :, None], wb, bb[:, :, None], wo, bo)
    return out[:, :K]


def neighbours(first, last, axis):
    peers = lax.axis_size(axis)
    up = [(i, i + 1) for i in range(peers - 1)]
    down = [(j, i) for i, j in up]
    return lax.ppermute(last, axis, up), lax.ppermute(first, axis, down)


def rims(tile):
    halo = BLOCKS * (D1 + D2)
    W = tile.shape[2]
    above, below = neighbours(tile[:, :halo], tile[:, -halo:], "rows")
    lane = jnp.arange(2 * halo)
    pick = jnp.where(lane < halo, lane, W - 2 * halo + lane)[:, None] == jnp.arange(W)[None, :]
    ends = jnp.einsum("dq,cpq->cdp", pick.astype(tile.dtype), tile, preferred_element_type=tile.dtype)
    left, right = neighbours(ends[:, :halo], ends[:, halo:], "cols")
    sides = jnp.concatenate([left, right], axis=1)
    up, down = neighbours(sides[:, :, :halo], sides[:, :, -halo:], "rows")
    corners = [jnp.swapaxes(v, 1, 2) for v in (up[:, :halo], up[:, halo:], down[:, :halo], down[:, halo:])]
    return above, below, left, right, corners


def shards(pair_maps, conv_a, bias_a, conv_b, bias_b, out_weight, out_bias):
    rows, cols = lax.axis_size("rows"), lax.axis_size("cols")
    _, C, H, W = pair_maps.shape
    halo = BLOCKS * (D1 + D2)
    r, c = lax.axis_index("rows"), lax.axis_index("cols")
    edge = jnp.stack([r == 0, r == rows - 1, c == 0, c == cols - 1]).astype(jnp.int32)
    tile = pair_maps[0]
    above, below, left, right, (ul, ur, dl, dr) = rims(tile)
    flip = functools.partial(jnp.swapaxes, axis1=1, axis2=2)
    flat = jnp.concatenate
    west, east = flat([flip(ul), left, flip(dl)], axis=2), flat([flip(ur), right, flip(dr)], axis=2)

    def caller(top, field, bottom, west, east, wa, wb, length):
        gap = jnp.zeros((C, 64 - 2 * halo, west.shape[2]), west.dtype)
        side = jnp.transpose(flat([west, east, gap], axis=1), (2, 0, 1))
        top, bottom = jnp.transpose(top, (1, 0, 2)), jnp.transpose(bottom, (1, 0, 2))
        return lambda info: chain(info, top, field, bottom, side, wa, bias_a, wb, bias_b, out_weight, out_bias, length)

    square_grid = rows == 4 and cols == 4 and H == W and H // rows == 64

    def merged(w):
        return w.reshape(BLOCKS, 3 * C, 3 * C)

    if square_grid:
        me = r * cols + c
        homes = plan(cols)
        turn, off = (jnp.array([homes.get((i // cols, i % cols), (0, 0, 0))[q] for i in range(rows * cols)])[me] for q in (1, 2))
        field = lax.cond(turn > 0, lambda v: jnp.transpose(v, (2, 0, 1)), lambda v: jnp.transpose(v, (1, 0, 2)), tile)
        north, south, west, east = (
            jnp.where(turn > 0, a, b)
            for a, b in ((left, above), (right, below), (flat([ul, above, ur], axis=2), west), (flat([dl, below, dr], axis=2), east))
        )
        edge = jnp.where(turn > 0, edge[jnp.array([2, 3, 0, 1])], edge)

        def turned(w):
            other = jnp.transpose(w.reshape(BLOCKS, 3, C, 3, C), (0, 3, 2, 1, 4))
            return jnp.where(turn > 0, merged(other), merged(w))

        wa, wb = turned(conv_a), turned(conv_b)
        q = cols // CHUNKS
        run = caller(north, field, south, west, east, wa, wb, H // CHUNKS)
        chunks, strips, recs = [], [], []
        for j in range(CHUNKS):
            info = jnp.append(edge, ((j * q) ^ (off & ~(q - 1))) * (H // cols))
            if j:
                info, *_ = lax.optimization_barrier((info, *strips[-q:]))
            chunks.append(jnp.transpose(run(info), (1, 0, 2)))
            for m in range(j * q, j * q + q):
                strips.append(lax.dynamic_slice_in_dim(chunks[j], ((m % q) ^ (off & (q - 1))) * (H // cols), H // cols, 1))
                perm = [(i * cols + k, home * cols + (m ^ o)) for (i, k), (home, _, o) in homes.items()]
                recs.append(lax.ppermute(strips[m], ("rows", "cols"), perm))
        return square(chunks, strips, recs)
    field = jnp.transpose(tile, (1, 0, 2))
    logits = caller(above, field, below, west, east, merged(conv_a), merged(conv_b), H)(jnp.append(edge, 0))
    logits = jnp.transpose(logits, (1, 0, 2))[None]
    strips = lax.all_to_all(logits, "cols", split_axis=2, concat_axis=3, tiled=True)
    flipped = lax.all_to_all(strips, ("rows", "cols"), split_axis=3, concat_axis=2, tiled=True)
    mirrored = jnp.swapaxes(flipped, 2, 3)
    symmetric = (strips.astype(jnp.float32) + mirrored.astype(jnp.float32)) * 0.5
    return symmetric - jnp.log(jnp.sum(jnp.exp(symmetric), axis=1, keepdims=True))


def pair_kernel(r0, r1, r2, r3, lab, msg):
    K, sub, lanes = r0.shape
    for p, (one, two) in enumerate(((r0, r2), (r1, r3))):

        def add(k, total, one=one, two=two, p=p):
            v = (one[k].astype(jnp.float32) + two[k].astype(jnp.float32)) * 0.5
            lab[p, k] = v
            return total + jnp.exp(v)

        norm = jnp.log(lax.fori_loop(0, K, add, jnp.zeros((sub, lanes), jnp.float32), unroll=4))

        def emit(k, carry, p=p, norm=norm):
            v = lab[p, k] - norm
            lab[p, k] = v
            w = v.T
            for t in range(lanes // sub):
                b = w[t * sub:(t + 1) * sub]
                msg[p, t, k] = jnp.concatenate([b[:sub // 2], b[sub // 2:]], axis=1).astype(jnp.bfloat16)
            return carry

        lax.fori_loop(0, K, emit, 0, unroll=4)


def pairs(recs):
    K, sub, W = recs[0].shape
    lanes = 128
    return pl.pallas_call(
        pair_kernel,
        grid=(W // lanes,),
        in_specs=[pl.BlockSpec((K, sub, lanes), lambda i: (0, 0, i))] * 4,
        out_specs=[
            pl.BlockSpec((2, K, sub, lanes), lambda i: (0, 0, 0, i)),
            pl.BlockSpec((2, lanes // sub, K, sub // 2, 2 * sub), lambda i: (0, i, 0, 0, 0)),
        ],
        out_shape=[
            jax.ShapeDtypeStruct((2, K, sub, W), jnp.float32),
            jax.ShapeDtypeStruct((2, W // sub, K, sub // 2, 2 * sub), jnp.bfloat16),
        ],
        name="pairs",
    )(*recs)


def own_kernel(a_ref, b_ref, o_ref, tmp):
    K = a_ref.shape[0]

    def add(k, total):
        v = (a_ref[k].astype(jnp.float32) + b_ref[k].astype(jnp.float32).T) * 0.5
        tmp[k] = v
        return total + jnp.exp(v)

    norm = jnp.log(lax.fori_loop(0, K, add, jnp.zeros(tmp.shape[1:], jnp.float32)))

    def emit(k, carry):
        o_ref[k] = (tmp[k] - norm).astype(jnp.bfloat16)
        return carry

    lax.fori_loop(0, K, emit, 0)


def own_pairs(tile):
    K, H, W = tile.shape
    B = 128
    return pl.pallas_call(
        own_kernel,
        grid=(H // B, W // B),
        in_specs=[pl.BlockSpec((K, B, B), lambda i, j: (0, i, j)), pl.BlockSpec((K, B, B), lambda i, j: (0, j, i))],
        out_specs=pl.BlockSpec((K, B, B), lambda i, j: (0, i, j)),
        out_shape=jax.ShapeDtypeStruct((K, H, W), jnp.bfloat16),
        scratch_shapes=[pltpu.VMEM((K, B, B), jnp.float32)],
        cost_estimate=pl.CostEstimate(flops=6 * K * H * W, bytes_accessed=6 * K * H * W, transcendentals=K * H * W),
        name="own",
    )(tile, tile)


def place_kernel(n, where_ref, diag, lab, *refs):
    o_ref = refs[-1]
    near, far = refs[:n], refs[n:2 * n]
    K, sub, W = diag.shape
    r, s = where_ref[0], where_ref[1]
    keeps = where_ref[2]

    def column(tile):
        return pl.multiple_of(lax.rem(tile, n) * W, W)

    def unpacked(source, k):
        parts = []
        for b in source:
            v = b[k].astype(jnp.float32)
            parts.append(jnp.concatenate([v[:, :sub], v[:, sub:]], axis=0))
        return parts

    def spread(source, k, tile):
        got = unpacked(source, k)
        for q in range(0, n, 2):
            pieces = []
            for b in (q, q + 1):
                v = got[0]
                for shift in range(1, n):
                    v = jnp.where(lax.rem(s + n - b, n) == shift, got[shift], v)
                pieces.append(v)
            o_ref[k, :, pl.ds(pl.multiple_of(column(tile) + q * sub, 2 * sub), 2 * sub)] = jnp.concatenate(pieces, axis=1)

    def body(k, carry):
        o_ref[k, :, pl.ds(column(r), W)] = diag[k].astype(jnp.float32)
        o_ref[k, :, pl.ds(column(r + 1), W)] = lab[lax.rem(s, 2), k]
        spread(near, k, r + n - 1)

        @pl.when(keeps > 0)
        def _():
            o_ref[k, :, pl.ds(column(r + 2), W)] = lab[1 - lax.rem(s, 2), k]

        @pl.when(keeps == 0)
        def _():
            spread(far, k, r + 2)

        return carry

    lax.fori_loop(0, K, body, 0)


def place(where, diag, lab, near, far):
    K, sub, W = diag.shape
    n = len(near)
    vm = pl.BlockSpec(memory_space=pltpu.VMEM)
    return pl.pallas_call(
        functools.partial(place_kernel, n),
        in_specs=[pl.BlockSpec(memory_space=pltpu.SMEM)] + [vm] * (2 + 2 * n),
        out_specs=vm,
        out_shape=jax.ShapeDtypeStruct((K, sub, n * W), jnp.float32),
        compiler_params=pltpu.CompilerParams(vmem_limit_bytes=40 * 1024 * 1024),
        name="place",
    )(where, diag, lab, *near, *far)


def plan(n):
    homes = {}
    for r in range(n):
        for c in range(n):
            gap = (c - r) % n
            if gap == 1:
                homes[r, c] = (r, 0, 0)
            elif gap == 3:
                homes[r, c] = (c, 1, 2)
            elif gap == 2:
                owner = 0 if 0 in (r, c) else 3
                homes[r, c] = (owner, int(r != owner), 1 if r == owner else 3)
    return homes


def square(chunks, strips, recs):
    n = lax.axis_size("rows")
    axes = ("rows", "cols")
    r, s = lax.axis_index("rows"), lax.axis_index("cols")
    sub = strips[0].shape[1]
    tile, *_ = lax.optimization_barrier((jnp.concatenate(chunks, axis=1), *strips))
    own = own_pairs(tile)
    diag = None
    for k in range(n):
        strip = lax.dynamic_slice_in_dim(own, lax.rem(r + k, n) * sub, sub, 1)
        if k == 0:
            diag = jnp.where(s == r, strip, jnp.zeros_like(strip))
        else:
            diag = diag + lax.ppermute(strip, axes, [(i * n + i, i * n + (i + k) % n) for i in range(n)])
    lab, msg = pairs(recs)
    near, far = [], []
    for k in range(n):
        t = lax.rem(s + k, n)
        for half, kept, moves in ((lax.rem(s, 2), near, [(i, (i + 1) % n) for i in range(n)]), (1 - lax.rem(s, 2), far, [(0, 2), (3, 1)])):
            payload = lax.dynamic_slice(msg, (half, t, 0, 0, 0), (1, 1) + msg.shape[2:])[0, 0]
            perm = [(i * n + j, o * n + (j + k) % n) for i, o in moves for j in range(n)]
            kept.append(lax.ppermute(payload, axes, perm))
    keeps = jnp.where((r == 0) | (r == n - 1), 1, 0)
    where = jnp.stack([r, s, keeps]).astype(jnp.int32)
    return place(where, diag, lab, near, far)[None]


def solution(mesh):
    in_specs = (P("crops", None, "rows", "cols"), P(), P(), P(), P(), P(), P())
    out_specs = P("crops", None, ("rows", "cols"), None)
    body = jax.shard_map(shards, mesh=mesh, in_specs=in_specs, out_specs=out_specs, check_vma=False)

    def run(*args):
        with jax.sharding.use_abstract_mesh(mesh.abstract_mesh):
            return body(*args)

    return run
```

```python
import functools

import jax
import jax.numpy as jnp
from jax import lax
from jax.experimental.layout import Layout, with_layout_constraint
from jax.experimental import pallas as pl
from jax.experimental.pallas import tpu as pltpu
from jax.sharding import PartitionSpec as P

BLOCKS = 2
D1 = 4
D2 = 8
CHUNKS = 2

FAR = 1 << 20
ROWS = 4
LEAD = 16


def chain_kernel(cfg, info_ref, t_ref, f_ref, b_ref, e_ref, wa_ref, ba_ref, wb_ref, bb_ref, wo_ref, bo_ref, o_ref, buf, side, sems, X, I, bias, acc, xa, xb):
    H, W, C, whole = cfg
    R = ROWS
    S = W + e_ref.shape[2]
    halo = BLOCKS * (D1 + D2)
    NB = R * S
    T = 256
    BF, F32 = jnp.bfloat16, jnp.float32
    start = info_ref[4]
    def moved(source, a, b, length, q):
        return pltpu.make_async_copy(source.at[pl.ds(a, length)], buf.at[pl.ds(b, length)], sems.at[q])

    middle = moved(f_ref, start, halo, H, 0)
    middle.start()
    sides = pltpu.make_async_copy(e_ref.at[pl.ds(start, H + 2 * halo)], side, sems.at[3])
    sides.start()
    for q, edge_ref, outer, a, b in ((1, t_ref, start == 0, start - halo, 0), (2, b_ref, start + H == whole, start + H, H + halo)):

        @pl.when(outer)
        def _(q=q, edge_ref=edge_ref, b=b):
            moved(edge_ref, 0, b, halo, q).start()

        @pl.when(jnp.logical_not(outer))
        def _(q=q, a=a, b=b):
            moved(f_ref, a, b, halo, q).start()

    def at(row):
        return pl.multiple_of(128 + (row + halo + LEAD) * S, 128)

    for k in range(BLOCKS):
        bias[2 * k] = jnp.broadcast_to(ba_ref[k], (C, 128))
        bias[2 * k + 1] = jnp.broadcast_to(bb_ref[k], (C, 128))
    middle.wait()
    sides.wait()
    moved(t_ref, 0, 0, halo, 1).wait()
    moved(b_ref, 0, H + halo, halo, 2).wait()

    def fill(i, _):
        parts = []
        for q in range(R):
            e = side[i * R + q]
            parts += [e[:, :halo], buf[i * R + q], e[:, halo:]]
        X[:, pl.ds(at(i * R - halo), NB)] = jnp.concatenate(parts, axis=1)
        return 0

    lax.fori_loop(0, (H + 2 * halo) // R, fill, 0)
    lane = lax.broadcasted_iota(jnp.int32, (8, NB), 1)
    col = lane % S
    dead = ((col < halo) & (info_ref[2] > 0)) | ((col >= halo + W) & (info_ref[3] > 0))
    rl = jnp.where(dead, 4 * FAR, lane // S)
    first = jnp.where(info_ref[0] > 0, -start, -FAR)
    last = jnp.where(info_ref[1] > 0, whole - start, FAR)

    def masked(v, row, t):
        p = rl[:, t:t + T]
        m = (p >= first - row) & (p < last - row)
        return jnp.where(m[None], v.reshape(C // 8, 8, T), 0.0).reshape(C, T)

    def biased(v, i):
        b = bias[i]
        return v + jnp.concatenate([b] * (T // 128), axis=1)

    def conv(src, d, w_ref, k, spare, emit):
        n = d // R
        ring = 2 * n + 1
        odd = H // R % 2
        lo = -spare - odd * R
        total = (H + 2 * spare) // R + odd + 2 * n

        def slot(j):
            return pl.multiple_of(lax.rem(j, ring) * NB, 128)

        def shift(j, xs):
            x = src[:, pl.ds(pl.multiple_of(at(lo - d + j * R) - 128, 128), NB + 256)]
            xs[0:C, :] = pltpu.roll(x, d, 1)[:, 128:128 + NB]
            xs[C:2 * C, :] = pltpu.roll(x, NB + 256 - d, 1)[:, 128:128 + NB]

        def step(j, xs, nxt):
            shift(j + 1, nxt)
            row = lo - d + j * R
            s0, s1, s2 = slot(j), slot(j + ring - n), slot(j + ring - 2 * n)
            for t in range(0, NB, T):
                x = jnp.concatenate([xs[0:C, t:t + T], src[:, pl.ds(at(row) + t, T)], xs[C:2 * C, t:t + T]], axis=0)
                y = jnp.dot(w_ref[k], x, preferred_element_type=F32)
                done = acc[:, pl.ds(s2 + t, T)] + y[2 * C:]
                acc[:, pl.ds(s1 + t, T)] += y[C:2 * C]
                acc[:, pl.ds(s0 + t, T)] = y[:C]
                emit(row - d, t, done)

        shift(0, xa)

        def body(i, _):
            step(2 * i, xa, xb)
            step(2 * i + 1, xb, xa)
            return 0

        lax.fori_loop(0, total // 2, body, 0)

    def block(k, carry):
        edge = (BLOCKS - k) * (D1 + D2)

        def emit_a(row, t, v):
            v = biased(v, 2 * k)
            e = jnp.where(v > 0, v, jnp.exp(v) - 1.0)
            I[:, pl.ds(at(row) + t, T)] = masked(e, row, t).astype(BF)

        conv(X, D1, wa_ref, k, edge - D1, emit_a)

        def emit_b(row, t, v):
            v = biased(v, 2 * k + 1) + X[:, pl.ds(at(row) + t, T)].astype(F32)
            X[:, pl.ds(at(row) + t, T)] = masked(v, row, t).astype(BF)

        conv(I, D2, wb_ref, k, edge - D1 - D2, emit_b)
        return carry

    lax.fori_loop(0, BLOCKS, block, 0)
    bo = jnp.broadcast_to(bo_ref[...], (bo_ref.shape[0], W))

    def project(i, _):
        x = X[:, pl.ds(at(i * R), NB)]
        for q in range(R):
            g = jnp.dot(wo_ref[...], x[:, q * S + halo:q * S + halo + W], preferred_element_type=F32) + bo
            o_ref[i * R + q] = g.astype(BF)
        return 0

    lax.fori_loop(0, H // R, project, 0)


def chain(info, top, field, bottom, side, wa, ba, wb, bb, wo, bo, H):
    whole, C, W = field.shape
    S = W + side.shape[2]
    K = wo.shape[0]
    R = ROWS
    halo = BLOCKS * (D1 + D2)
    N = 128 + (H + 2 * halo + LEAD + R) * S + 256
    KP = -(-K // 16) * 16
    wo = jnp.pad(wo, ((0, KP - K), (0, 0)))
    bo = jnp.pad(bo, (0, KP - K))[:, None]
    vm = pl.BlockSpec(memory_space=pltpu.VMEM)
    ring = (2 * (max(D1, D2) // R) + 1) * R * S
    flops = 2 * BLOCKS * 2 * 9 * C * C * H * S
    out = pl.pallas_call(
        functools.partial(chain_kernel, (H, W, C, whole)),
        out_shape=jax.ShapeDtypeStruct((H, KP, W), jnp.bfloat16),
        in_specs=[pl.BlockSpec(memory_space=pltpu.SMEM), *[pl.BlockSpec(memory_space=pltpu.HBM)] * 4] + [vm] * 6,
        out_specs=vm,
        scratch_shapes=[
            pltpu.VMEM((H + 2 * halo, C, W), jnp.bfloat16),
            pltpu.VMEM((H + 2 * halo, C, S - W), jnp.bfloat16),
            pltpu.SemaphoreType.DMA((4,)),
            pltpu.VMEM((C, N), jnp.bfloat16),
            pltpu.VMEM((C, N), jnp.bfloat16),
            pltpu.VMEM((2 * BLOCKS, C, 128), jnp.float32),
            pltpu.VMEM((C, ring), jnp.float32),
            pltpu.VMEM((2 * C, R * S), jnp.bfloat16),
            pltpu.VMEM((2 * C, R * S), jnp.bfloat16),
        ],
        compiler_params=pltpu.CompilerParams(vmem_limit_bytes=63000 * 1024),
        cost_estimate=pl.CostEstimate(flops=flops, bytes_accessed=4 * C * H * S, transcendentals=2 * C * H * S),
        name="chain",
    )(info, top, field, bottom, side, wa, ba[:, :, None], wb, bb[:, :, None], wo, bo)
    return out[:, :K]


def neighbours(first, last, axis):
    peers = lax.axis_size(axis)
    up = [(i, i + 1) for i in range(peers - 1)]
    down = [(j, i) for i, j in up]
    return lax.ppermute(last, axis, up), lax.ppermute(first, axis, down)


def rims(tile):
    halo = BLOCKS * (D1 + D2)
    W = tile.shape[2]
    above, below = neighbours(tile[:, :halo], tile[:, -halo:], "rows")
    lane = jnp.arange(2 * halo)
    pick = jnp.where(lane < halo, lane, W - 2 * halo + lane)[:, None] == jnp.arange(W)[None, :]
    ends = jnp.einsum("dq,cpq->cdp", pick.astype(tile.dtype), tile, preferred_element_type=tile.dtype)
    left, right = neighbours(ends[:, :halo], ends[:, halo:], "cols")
    sides = jnp.concatenate([left, right], axis=1)
    up, down = neighbours(sides[:, :, :halo], sides[:, :, -halo:], "rows")
    corners = [jnp.swapaxes(v, 1, 2) for v in (up[:, :halo], up[:, halo:], down[:, :halo], down[:, halo:])]
    return above, below, left, right, corners


def shards(pair_maps, conv_a, bias_a, conv_b, bias_b, out_weight, out_bias):
    rows, cols = lax.axis_size("rows"), lax.axis_size("cols")
    _, C, H, W = pair_maps.shape
    halo = BLOCKS * (D1 + D2)
    r, c = lax.axis_index("rows"), lax.axis_index("cols")
    edge = jnp.stack([r == 0, r == rows - 1, c == 0, c == cols - 1]).astype(jnp.int32)
    tile = pair_maps[0]
    above, below, left, right, (ul, ur, dl, dr) = rims(tile)
    flip = functools.partial(jnp.swapaxes, axis1=1, axis2=2)
    flat = jnp.concatenate
    west, east = flat([flip(ul), left, flip(dl)], axis=2), flat([flip(ur), right, flip(dr)], axis=2)

    def caller(top, field, bottom, west, east, wa, wb, length):
        gap = jnp.zeros((C, 64 - 2 * halo, west.shape[2]), west.dtype)
        west, east, top, bottom = (with_layout_constraint(v, Layout((0, 1, 2))) for v in (west, east, top, bottom))
        side = with_layout_constraint(flat([west, east, gap], axis=1), Layout((0, 1, 2)))
        side, top, bottom = lax.optimization_barrier((side, top, bottom))
        side, top, bottom = jnp.transpose(side, (2, 0, 1)), jnp.transpose(top, (1, 0, 2)), jnp.transpose(bottom, (1, 0, 2))
        return lambda info: chain(info, top, field, bottom, side, wa, bias_a, wb, bias_b, out_weight, out_bias, length)

    square_grid = rows == 4 and cols == 4 and H == W and H // rows == 64

    def merged(w):
        return w.reshape(BLOCKS, 3 * C, 3 * C)

    if square_grid:
        me = r * cols + c
        homes = plan(cols)
        turn, off = (jnp.array([homes.get((i // cols, i % cols), (0, 0, 0))[q] for i in range(rows * cols)])[me] for q in (1, 2))
        field = lax.cond(turn > 0, lambda v: jnp.transpose(v, (2, 0, 1)), lambda v: jnp.transpose(v, (1, 0, 2)), tile)
        north, south, west, east = (
            jnp.where(turn > 0, a, b)
            for a, b in ((left, above), (right, below), (flat([ul, above, ur], axis=2), west), (flat([dl, below, dr], axis=2), east))
        )
        edge = jnp.where(turn > 0, edge[jnp.array([2, 3, 0, 1])], edge)

        def turned(w):
            other = jnp.transpose(w.reshape(BLOCKS, 3, C, 3, C), (0, 3, 2, 1, 4))
            return jnp.where(turn > 0, merged(other), merged(w))

        wa, wb = turned(conv_a), turned(conv_b)
        q = cols // CHUNKS
        run = caller(north, field, south, west, east, wa, wb, H // CHUNKS)
        chunks, strips, recs = [], [], []
        for j in range(CHUNKS):
            info = jnp.append(edge, ((j * q) ^ (off & ~(q - 1))) * (H // cols))
            if j:
                info, *_ = lax.optimization_barrier((info, *strips[-q:]))
            chunks.append(jnp.transpose(run(info), (1, 0, 2)))
            for m in range(j * q, j * q + q):
                strips.append(lax.dynamic_slice_in_dim(chunks[j], ((m % q) ^ (off & (q - 1))) * (H // cols), H // cols, 1))
                perm = [(i * cols + k, home * cols + (m ^ o)) for (i, k), (home, _, o) in homes.items()]
                recs.append(lax.ppermute(strips[m], ("rows", "cols"), perm))
        return square(chunks, strips, recs)
    field = jnp.transpose(tile, (1, 0, 2))
    logits = caller(above, field, below, west, east, merged(conv_a), merged(conv_b), H)(jnp.append(edge, 0))
    logits = jnp.transpose(logits, (1, 0, 2))[None]
    strips = lax.all_to_all(logits, "cols", split_axis=2, concat_axis=3, tiled=True)
    flipped = lax.all_to_all(strips, ("rows", "cols"), split_axis=3, concat_axis=2, tiled=True)
    mirrored = jnp.swapaxes(flipped, 2, 3)
    symmetric = (strips.astype(jnp.float32) + mirrored.astype(jnp.float32)) * 0.5
    return symmetric - jnp.log(jnp.sum(jnp.exp(symmetric), axis=1, keepdims=True))


def pair_kernel(n, where_ref, r0, r1, r2, r3, o_ref, msg, lab, sems):
    K, sub, lanes = r0.shape
    r, s, keeps = where_ref[0], where_ref[1], where_ref[2]
    g = pl.program_id(0)
    W = lanes * pl.num_programs(0)

    def out(p, tile):
        spot = pl.multiple_of(lax.rem(tile, n) * W + g * lanes, lanes)
        return pltpu.make_async_copy(lab.at[p], o_ref.at[:, :, pl.ds(spot, lanes)], sems.at[p])

    for p, (one, two) in enumerate(((r0, r2), (r1, r3))):
        total = jnp.zeros((sub, lanes), jnp.float32)
        for k in range(K):
            v = (one[k].astype(jnp.float32) + two[k].astype(jnp.float32)) * 0.5
            lab[p, k] = v
            total = total + jnp.exp(v)
        norm = jnp.log(total)
        for k in range(K):
            v = lab[p, k] - norm
            lab[p, k] = v
            w = v.T
            for t in range(lanes // sub):
                b = w[t * sub:(t + 1) * sub]
                msg[p, t, k] = jnp.concatenate([b[:sub // 2], b[sub // 2:]], axis=1).astype(jnp.bfloat16)

        @pl.when(lax.rem(s, 2) == p)
        def _(p=p):
            out(p, r + 1).start()

        @pl.when((lax.rem(s, 2) != p) & (keeps > 0))
        def _(p=p):
            out(p, r + 2).start()

    for p in range(2):

        @pl.when((lax.rem(s, 2) == p) | (keeps > 0))
        def _(p=p):
            out(p, 0).wait()


def pairs(where, recs):
    K, sub, W = recs[0].shape
    lanes, n = 128, len(recs)
    return pl.pallas_call(
        functools.partial(pair_kernel, n),
        grid=(W // lanes,),
        in_specs=[pl.BlockSpec(memory_space=pltpu.SMEM)] + [pl.BlockSpec((K, sub, lanes), lambda i: (0, 0, i))] * 4,
        out_specs=[
            pl.BlockSpec(memory_space=pltpu.HBM),
            pl.BlockSpec((2, lanes // sub, K, sub // 2, 2 * sub), lambda i: (0, i, 0, 0, 0)),
        ],
        out_shape=[
            jax.ShapeDtypeStruct((K, sub, n * W), jnp.float32),
            jax.ShapeDtypeStruct((2, W // sub, K, sub // 2, 2 * sub), jnp.bfloat16),
        ],
        scratch_shapes=[pltpu.VMEM((2, K, sub, lanes), jnp.float32), pltpu.SemaphoreType.DMA((2,))],
        name="pairs",
    )(where, *recs)


def own_kernel(a_ref, b_ref, o_ref, tmp):
    K = a_ref.shape[0]

    def add(k, total):
        v = (a_ref[k].astype(jnp.float32) + b_ref[k].astype(jnp.float32).T) * 0.5
        tmp[k] = v
        return total + jnp.exp(v)

    norm = jnp.log(lax.fori_loop(0, K, add, jnp.zeros(tmp.shape[1:], jnp.float32), unroll=2))

    def emit(k, carry):
        o_ref[k] = (tmp[k] - norm).astype(jnp.bfloat16)
        return carry

    lax.fori_loop(0, K, emit, 0, unroll=2)


def own_pairs(tile):
    K, H, W = tile.shape
    B = 128
    return pl.pallas_call(
        own_kernel,
        grid=(H // B, W // B),
        in_specs=[pl.BlockSpec((K, B, B), lambda i, j: (0, i, j)), pl.BlockSpec((K, B, B), lambda i, j: (0, j, i))],
        out_specs=pl.BlockSpec((K, B, B), lambda i, j: (0, i, j)),
        out_shape=jax.ShapeDtypeStruct((K, H, W), jnp.bfloat16),
        scratch_shapes=[pltpu.VMEM((K, B, B), jnp.float32)],
        cost_estimate=pl.CostEstimate(flops=6 * K * H * W, bytes_accessed=6 * K * H * W, transcendentals=K * H * W),
        name="own",
    )(tile, tile)


def place_kernel(n, where_ref, diag, near, far, _, o_ref, own, one, two, sems):
    K, sub, W = diag.shape
    r, s, keeps = where_ref[0], where_ref[1], where_ref[2]

    def out(source, tile, q):
        spot = pl.multiple_of(lax.rem(tile, n) * W, W)
        return pltpu.make_async_copy(source, o_ref.at[:, :, pl.ds(spot, W)], sems.at[q])

    def spread(source, target):
        def body(k, carry):
            pieces = []
            for b in range(n):
                v = source[lax.rem(s + n - b, n), k].astype(jnp.float32)
                pieces.append(jnp.concatenate([v[:, :sub], v[:, sub:]], axis=0))
            target[k] = jnp.concatenate(pieces, axis=1)
            return carry

        lax.fori_loop(0, K, body, 0, unroll=4)

    def widen(k, carry):
        own[k] = diag[k].astype(jnp.float32)
        return carry

    lax.fori_loop(0, K, widen, 0, unroll=4)
    out(own, r, 0).start()
    spread(near, one)
    out(one, r + n - 1, 1).start()

    @pl.when(keeps == 0)
    def _():
        spread(far, two)
        out(two, r + 2, 2).start()
        out(two, r + 2, 2).wait()

    out(own, r, 0).wait()
    out(one, r + n - 1, 1).wait()


def place(where, diag, near, far, result):
    K, sub, W = diag.shape
    n = near.shape[0]
    vm = pl.BlockSpec(memory_space=pltpu.VMEM)
    hbm = pl.BlockSpec(memory_space=pltpu.HBM)
    return pl.pallas_call(
        functools.partial(place_kernel, n),
        in_specs=[pl.BlockSpec(memory_space=pltpu.SMEM), vm, vm, vm, hbm],
        out_specs=hbm,
        out_shape=jax.ShapeDtypeStruct((K, sub, n * W), jnp.float32),
        input_output_aliases={4: 0},
        scratch_shapes=[pltpu.VMEM((K, sub, W), jnp.float32)] * 3 + [pltpu.SemaphoreType.DMA((3,))],
        compiler_params=pltpu.CompilerParams(vmem_limit_bytes=40 * 1024 * 1024),
        name="place",
    )(where, diag, near, far, result)


def plan(n):
    homes = {}
    for r in range(n):
        for c in range(n):
            gap = (c - r) % n
            if gap == 1:
                homes[r, c] = (r, 0, 0)
            elif gap == 3:
                homes[r, c] = (c, 1, 2)
            elif gap == 2:
                owner = 0 if 0 in (r, c) else 3
                homes[r, c] = (owner, int(r != owner), 1 if r == owner else 3)
    return homes


def square(chunks, strips, recs):
    n = lax.axis_size("rows")
    axes = ("rows", "cols")
    r, s = lax.axis_index("rows"), lax.axis_index("cols")
    sub = strips[0].shape[1]
    tile, *_ = lax.optimization_barrier((jnp.concatenate(chunks, axis=1), *strips))
    own = own_pairs(tile)
    diag = None
    for k in range(n):
        strip = lax.dynamic_slice_in_dim(own, lax.rem(r + k, n) * sub, sub, 1)
        if k == 0:
            diag = jnp.where(s == r, strip, jnp.zeros_like(strip))
        else:
            diag = diag + lax.ppermute(strip, axes, [(i * n + i, i * n + (i + k) % n) for i in range(n)])
    keeps = jnp.where((r == 0) | (r == n - 1), 1, 0)
    where = jnp.stack([r, s, keeps]).astype(jnp.int32)
    result, msg = pairs(where, recs)
    near, far = [], []
    for k in range(n):
        t = lax.rem(s + k, n)
        for half, kept, moves in ((lax.rem(s, 2), near, [(i, (i + 1) % n) for i in range(n)]), (1 - lax.rem(s, 2), far, [(0, 2), (3, 1)])):
            payload = lax.dynamic_slice(msg, (half, t, 0, 0, 0), (1, 1) + msg.shape[2:])[0, 0]
            perm = [(i * n + j, o * n + (j + k) % n) for i, o in moves for j in range(n)]
            kept.append(lax.ppermute(payload, axes, perm))
    return place(where, diag, jnp.stack(near), jnp.stack(far), result)[None]


def solution(mesh):
    in_specs = (P("crops", None, "rows", "cols"), P(), P(), P(), P(), P(), P())
    out_specs = P("crops", None, ("rows", "cols"), None)
    body = jax.shard_map(shards, mesh=mesh, in_specs=in_specs, out_specs=out_specs, check_vma=False)

    def run(*args):
        with jax.sharding.use_abstract_mesh(mesh.abstract_mesh):
            return body(*args)

    return run
```

```python
import functools

import jax
import jax.numpy as jnp
from jax import lax
from jax.experimental.layout import Layout, with_layout_constraint
from jax.experimental import pallas as pl
from jax.experimental.pallas import tpu as pltpu
from jax.sharding import PartitionSpec as P


BLOCKS = 2
D1 = 4
D2 = 8
CHUNKS = 2

FAR = 1 << 20
ROWS = 4
LEAD = 16


def chain_kernel(cfg, info_ref, t_ref, f_ref, b_ref, e_ref, wa_ref, ba_ref, wb_ref, bb_ref, wo_ref, bo_ref, o_ref, buf, side, sems, X, I, bias, acc, xa, xb):
    H, W, C, whole = cfg
    R = ROWS
    S = W + e_ref.shape[2]
    halo = BLOCKS * (D1 + D2)
    NB = R * S
    T = 256
    BF, F32 = jnp.bfloat16, jnp.float32
    start = info_ref[4]

    def moved(source, a, b, length, q):
        return pltpu.make_async_copy(source.at[pl.ds(a, length)], buf.at[pl.ds(b, length)], sems.at[q])

    middle = moved(f_ref, start, halo, H, 0)
    middle.start()
    sides = pltpu.make_async_copy(e_ref.at[pl.ds(start, H + 2 * halo)], side, sems.at[3])
    sides.start()
    for q, edge_ref, outer, a, b in ((1, t_ref, start == 0, start - halo, 0), (2, b_ref, start + H == whole, start + H, H + halo)):

        @pl.when(outer)
        def _(q=q, edge_ref=edge_ref, b=b):
            moved(edge_ref, 0, b, halo, q).start()

        @pl.when(jnp.logical_not(outer))
        def _(q=q, a=a, b=b):
            moved(f_ref, a, b, halo, q).start()

    def at(row):
        return pl.multiple_of(128 + (row + halo + LEAD) * S, 128)

    for k in range(BLOCKS):
        bias[2 * k] = jnp.broadcast_to(ba_ref[k], (C, 128))
        bias[2 * k + 1] = jnp.broadcast_to(bb_ref[k], (C, 128))
    middle.wait()
    sides.wait()
    moved(t_ref, 0, 0, halo, 1).wait()
    moved(b_ref, 0, H + halo, halo, 2).wait()

    def fill(i, _):
        parts = []
        for q in range(R):
            e = side[i * R + q]
            parts += [e[:, :halo], buf[i * R + q], e[:, halo:]]
        X[:, pl.ds(at(i * R - halo), NB)] = jnp.concatenate(parts, axis=1)
        return 0

    lax.fori_loop(0, (H + 2 * halo) // R, fill, 0)
    lane = lax.broadcasted_iota(jnp.int32, (8, NB), 1)
    col = lane % S
    dead = ((col < halo) & (info_ref[2] > 0)) | ((col >= halo + W) & (info_ref[3] > 0))
    rl = jnp.where(dead, 4 * FAR, lane // S)
    first = jnp.where(info_ref[0] > 0, -start, -FAR)
    last = jnp.where(info_ref[1] > 0, whole - start, FAR)

    def masked(v, row, t):
        p = rl[:, t:t + T]
        m = (p >= first - row) & (p < last - row)
        return jnp.where(m[None], v.reshape(C // 8, 8, T), 0.0).reshape(C, T)

    def biased(v, i):
        b = bias[i]
        return v + jnp.concatenate([b] * (T // 128), axis=1)

    def conv(src, d, w_ref, k, spare, emit):
        n = d // R
        ring = 2 * n + 1
        odd = H // R % 2
        lo = -spare - odd * R
        total = (H + 2 * spare) // R + odd + 2 * n

        def slot(j):
            return pl.multiple_of(lax.rem(j, ring) * NB, 128)

        def shift(j, xs):
            x = src[:, pl.ds(pl.multiple_of(at(lo - d + j * R) - 128, 128), NB + 256)]
            xs[0:C, :] = pltpu.roll(x, d, 1)[:, 128:128 + NB]
            xs[C:2 * C, :] = pltpu.roll(x, NB + 256 - d, 1)[:, 128:128 + NB]

        def step(j, xs, nxt):
            shift(j + 1, nxt)
            row = lo - d + j * R
            s0, s1, s2 = slot(j), slot(j + ring - n), slot(j + ring - 2 * n)
            for t in range(0, NB, T):
                x = jnp.concatenate([xs[0:C, t:t + T], src[:, pl.ds(at(row) + t, T)], xs[C:2 * C, t:t + T]], axis=0)
                y = jnp.dot(w_ref[k], x, preferred_element_type=F32)
                done = acc[:, pl.ds(s2 + t, T)] + y[2 * C:]
                acc[:, pl.ds(s1 + t, T)] += y[C:2 * C]
                acc[:, pl.ds(s0 + t, T)] = y[:C]
                emit(row - d, t, done)

        shift(0, xa)

        def body(i, _):
            step(2 * i, xa, xb)
            step(2 * i + 1, xb, xa)
            return 0

        lax.fori_loop(0, total // 2, body, 0)

    def block(k, carry):
        edge = (BLOCKS - k) * (D1 + D2)

        def emit_a(row, t, v):
            v = biased(v, 2 * k)
            e = jnp.where(v > 0, v, jnp.exp(v) - 1.0)
            I[:, pl.ds(at(row) + t, T)] = masked(e, row, t).astype(BF)

        conv(X, D1, wa_ref, k, edge - D1, emit_a)

        def emit_b(row, t, v):
            v = biased(v, 2 * k + 1) + X[:, pl.ds(at(row) + t, T)].astype(F32)
            X[:, pl.ds(at(row) + t, T)] = masked(v, row, t).astype(BF)

        conv(I, D2, wb_ref, k, edge - D1 - D2, emit_b)
        return carry

    lax.fori_loop(0, BLOCKS, block, 0)
    bo = jnp.broadcast_to(bo_ref[...], (bo_ref.shape[0], W))

    def project(i, _):
        x = X[:, pl.ds(at(i * R), NB)]
        for q in range(R):
            g = jnp.dot(wo_ref[...], x[:, q * S + halo:q * S + halo + W], preferred_element_type=F32) + bo
            o_ref[i * R + q] = g.astype(BF)
        return 0

    lax.fori_loop(0, H // R, project, 0)


def chain(info, top, field, bottom, side, wa, ba, wb, bb, wo, bo, H):
    whole, C, W = field.shape
    S = W + side.shape[2]
    K = wo.shape[0]
    R = ROWS
    halo = BLOCKS * (D1 + D2)
    N = 128 + (H + 2 * halo + LEAD + R) * S + 256
    KP = -(-K // 16) * 16
    wo = jnp.pad(wo, ((0, KP - K), (0, 0)))
    bo = jnp.pad(bo, (0, KP - K))[:, None]
    vm = pl.BlockSpec(memory_space=pltpu.VMEM)
    ring = (2 * (max(D1, D2) // R) + 1) * R * S
    flops = 2 * BLOCKS * 2 * 9 * C * C * H * S
    out = pl.pallas_call(
        functools.partial(chain_kernel, (H, W, C, whole)),
        out_shape=jax.ShapeDtypeStruct((H, KP, W), jnp.bfloat16),
        in_specs=[pl.BlockSpec(memory_space=pltpu.SMEM), *[pl.BlockSpec(memory_space=pltpu.HBM)] * 4] + [vm] * 6,
        out_specs=vm,
        scratch_shapes=[
            pltpu.VMEM((H + 2 * halo, C, W), jnp.bfloat16),
            pltpu.VMEM((H + 2 * halo, C, S - W), jnp.bfloat16),
            pltpu.SemaphoreType.DMA((4,)),
            pltpu.VMEM((C, N), jnp.bfloat16),
            pltpu.VMEM((C, N), jnp.bfloat16),
            pltpu.VMEM((2 * BLOCKS, C, 128), jnp.float32),
            pltpu.VMEM((C, ring), jnp.float32),
            pltpu.VMEM((2 * C, R * S), jnp.bfloat16),
            pltpu.VMEM((2 * C, R * S), jnp.bfloat16),
        ],
        compiler_params=pltpu.CompilerParams(vmem_limit_bytes=63000 * 1024),
        cost_estimate=pl.CostEstimate(flops=flops, bytes_accessed=4 * C * H * S, transcendentals=2 * C * H * S),
        name="chain",
    )(info, top, field, bottom, side, wa, ba[:, :, None], wb, bb[:, :, None], wo, bo)
    return out[:, :K]


def neighbours(first, last, axis):
    peers = lax.axis_size(axis)
    up = [(i, i + 1) for i in range(peers - 1)]
    down = [(j, i) for i, j in up]
    return lax.ppermute(last, axis, up), lax.ppermute(first, axis, down)


def rims(tile):
    halo = BLOCKS * (D1 + D2)
    W = tile.shape[2]
    above, below = neighbours(tile[:, :halo], tile[:, -halo:], "rows")
    lane = jnp.arange(2 * halo)
    pick = jnp.where(lane < halo, lane, W - 2 * halo + lane)[:, None] == jnp.arange(W)[None, :]
    ends = jnp.einsum("dq,cpq->cdp", pick.astype(tile.dtype), tile, preferred_element_type=tile.dtype)
    left, right = neighbours(ends[:, :halo], ends[:, halo:], "cols")
    sides = jnp.concatenate([left, right], axis=1)
    up, down = neighbours(sides[:, :, :halo], sides[:, :, -halo:], "rows")
    corners = jnp.stack([up[:, :halo], up[:, halo:], down[:, :halo], down[:, halo:]], axis=1)
    return above, below, left, right, corners


def shards(pair_maps, conv_a, bias_a, conv_b, bias_b, out_weight, out_bias):
    rows, cols = lax.axis_size("rows"), lax.axis_size("cols")
    _, C, H, W = pair_maps.shape
    halo = BLOCKS * (D1 + D2)
    r, c = lax.axis_index("rows"), lax.axis_index("cols")
    edge = jnp.stack([r == 0, r == rows - 1, c == 0, c == cols - 1]).astype(jnp.int32)
    tile = pair_maps[0]
    above, below, left, right, corners = rims(tile)
    flat = jnp.concatenate

    def sides(left, right, corners, second, third):
        west = flat([corners[:, 0], left, corners[:, third]], axis=2)
        east = flat([corners[:, second], right, corners[:, 3]], axis=2)
        return west, east

    def caller(top, field, bottom, west, east, wa, wb, length):
        gap = jnp.zeros((C, 64 - 2 * halo, west.shape[2]), west.dtype)
        west, east, top, bottom = (with_layout_constraint(v, Layout((0, 1, 2))) for v in (west, east, top, bottom))
        side = with_layout_constraint(flat([west, east, gap], axis=1), Layout((0, 1, 2)))
        side, top, bottom = lax.optimization_barrier((side, top, bottom))
        side, top, bottom = jnp.transpose(side, (2, 0, 1)), jnp.transpose(top, (1, 0, 2)), jnp.transpose(bottom, (1, 0, 2))
        return lambda info: chain(info, top, field, bottom, side, wa, bias_a, wb, bias_b, out_weight, out_bias, length)

    square_grid = rows == 4 and cols == 4 and H == W and H // rows == 64

    def merged(w):
        return w.reshape(BLOCKS, 3 * C, 3 * C)

    if square_grid:
        me = r * cols + c
        homes = plan(cols)
        turn, off = (jnp.array([homes.get((i // cols, i % cols), (0, 0, 0))[q] for i in range(rows * cols)])[me] for q in (1, 2))
        field = lax.cond(turn > 0, lambda v: jnp.transpose(v, (2, 0, 1)), lambda v: jnp.transpose(v, (1, 0, 2)), tile)
        fixed = with_layout_constraint(jnp.swapaxes(corners, 2, 3), Layout((0, 1, 2, 3)))
        corners = jnp.where(turn > 0, fixed[:, jnp.array([0, 2, 1, 3])], with_layout_constraint(corners, Layout((0, 1, 2, 3))))
        north, south, west, east = (jnp.where(turn > 0, a, b) for a, b in ((left, above), (right, below), (above, left), (below, right)))
        west, east = sides(west, east, corners, 1, 2)
        edge = jnp.where(turn > 0, edge[jnp.array([2, 3, 0, 1])], edge)

        def turned(w):
            other = jnp.transpose(w.reshape(BLOCKS, 3, C, 3, C), (0, 3, 2, 1, 4))
            return jnp.where(turn > 0, merged(other), merged(w))

        wa, wb = turned(conv_a), turned(conv_b)
        q = cols // CHUNKS
        run = caller(north, field, south, west, east, wa, wb, H // CHUNKS)
        chunks, strips, recs = [], [], []
        for j in range(CHUNKS):
            info = jnp.append(edge, ((j * q) ^ (off & ~(q - 1))) * (H // cols))
            if j:
                info, *_ = lax.optimization_barrier((info, *strips[-q:]))
            chunks.append(jnp.transpose(run(info), (1, 0, 2)))
            for m in range(j * q, j * q + q):
                strips.append(lax.dynamic_slice_in_dim(chunks[j], ((m % q) ^ (off & (q - 1))) * (H // cols), H // cols, 1))
                perm = [(i * cols + k, home * cols + (m ^ o)) for (i, k), (home, _, o) in homes.items()]
                recs.append(lax.ppermute(strips[m], ("rows", "cols"), perm))
        return square(chunks, strips, recs)
    field = jnp.transpose(tile, (1, 0, 2))
    west, east = sides(left, right, corners, 1, 2)
    logits = caller(above, field, below, west, east, merged(conv_a), merged(conv_b), H)(jnp.append(edge, 0))
    logits = jnp.transpose(logits, (1, 0, 2))[None]
    strips = lax.all_to_all(logits, "cols", split_axis=2, concat_axis=3, tiled=True)
    flipped = lax.all_to_all(strips, ("rows", "cols"), split_axis=3, concat_axis=2, tiled=True)
    mirrored = jnp.swapaxes(flipped, 2, 3)
    symmetric = (strips.astype(jnp.float32) + mirrored.astype(jnp.float32)) * 0.5
    return symmetric - jnp.log(jnp.sum(jnp.exp(symmetric), axis=1, keepdims=True))


def pair_kernel(n, where_ref, r0, r1, r2, r3, o_ref, msg, lab, sems):
    K, sub, lanes = r0.shape
    r, s, keeps = where_ref[0], where_ref[1], where_ref[2]
    g = pl.program_id(0)
    W = lanes * pl.num_programs(0)

    def out(p, tile):
        spot = pl.multiple_of(lax.rem(tile, n) * W + g * lanes, lanes)
        return pltpu.make_async_copy(lab.at[p], o_ref.at[:, :, pl.ds(spot, lanes)], sems.at[p])

    for p, (one, two) in enumerate(((r0, r2), (r1, r3))):
        total = jnp.zeros((sub, lanes), jnp.float32)
        for k in range(K):
            v = (one[k].astype(jnp.float32) + two[k].astype(jnp.float32)) * 0.5
            lab[p, k] = v
            total = total + jnp.exp(v)
        norm = jnp.log(total)
        for k in range(K):
            v = lab[p, k] - norm
            lab[p, k] = v
            w = v.T
            for t in range(lanes // sub):
                b = w[t * sub:(t + 1) * sub]
                msg[p, t, k] = jnp.concatenate([b[:sub // 2], b[sub // 2:]], axis=1).astype(jnp.bfloat16)

        @pl.when(lax.rem(s, 2) == p)
        def _(p=p):
            out(p, r + 1).start()

        @pl.when((lax.rem(s, 2) != p) & (keeps > 0))
        def _(p=p):
            out(p, r + 2).start()

    for p in range(2):

        @pl.when((lax.rem(s, 2) == p) | (keeps > 0))
        def _(p=p):
            out(p, 0).wait()


def pairs(where, recs):
    K, sub, W = recs[0].shape
    lanes, n = 128, len(recs)
    return pl.pallas_call(
        functools.partial(pair_kernel, n),
        grid=(W // lanes,),
        in_specs=[pl.BlockSpec(memory_space=pltpu.SMEM)] + [pl.BlockSpec((K, sub, lanes), lambda i: (0, 0, i))] * 4,
        out_specs=[
            pl.BlockSpec(memory_space=pltpu.HBM),
            pl.BlockSpec((2, lanes // sub, K, sub // 2, 2 * sub), lambda i: (0, i, 0, 0, 0)),
        ],
        out_shape=[
            jax.ShapeDtypeStruct((K, sub, n * W), jnp.float32),
            jax.ShapeDtypeStruct((2, W // sub, K, sub // 2, 2 * sub), jnp.bfloat16),
        ],
        scratch_shapes=[pltpu.VMEM((2, K, sub, lanes), jnp.float32), pltpu.SemaphoreType.DMA((2,))],
        name="pairs",
    )(where, *recs)


def own_kernel(a_ref, b_ref, o_ref, tmp):
    K = a_ref.shape[0]

    def add(k, total):
        v = (a_ref[k].astype(jnp.float32) + b_ref[k].astype(jnp.float32).T) * 0.5
        tmp[k] = v
        return total + jnp.exp(v)

    norm = jnp.log(lax.fori_loop(0, K, add, jnp.zeros(tmp.shape[1:], jnp.float32), unroll=2))

    def emit(k, carry):
        o_ref[k] = (tmp[k] - norm).astype(jnp.bfloat16)
        return carry

    lax.fori_loop(0, K, emit, 0, unroll=2)


def own_pairs(tile):
    K, H, W = tile.shape
    B = 128
    return pl.pallas_call(
        own_kernel,
        grid=(H // B, W // B),
        in_specs=[pl.BlockSpec((K, B, B), lambda i, j: (0, i, j)), pl.BlockSpec((K, B, B), lambda i, j: (0, j, i))],
        out_specs=pl.BlockSpec((K, B, B), lambda i, j: (0, i, j)),
        out_shape=jax.ShapeDtypeStruct((K, H, W), jnp.bfloat16),
        scratch_shapes=[pltpu.VMEM((K, B, B), jnp.float32)],
        cost_estimate=pl.CostEstimate(flops=6 * K * H * W, bytes_accessed=6 * K * H * W, transcendentals=K * H * W),
        name="own",
    )(tile, tile)


def place_kernel(n, where_ref, diag, near, far, _, o_ref, own, one, two, sems):
    K, sub, W = diag.shape
    r, s, keeps = where_ref[0], where_ref[1], where_ref[2]

    def out(source, tile, q):
        spot = pl.multiple_of(lax.rem(tile, n) * W, W)
        return pltpu.make_async_copy(source, o_ref.at[:, :, pl.ds(spot, W)], sems.at[q])

    def spread(source, target):
        def body(k, carry):
            pieces = []
            for b in range(n):
                v = source[lax.rem(s + n - b, n), k].astype(jnp.float32)
                pieces.append(jnp.concatenate([v[:, :sub], v[:, sub:]], axis=0))
            target[k] = jnp.concatenate(pieces, axis=1)
            return carry

        lax.fori_loop(0, K, body, 0, unroll=4)

    def widen(k, carry):
        own[k] = diag[k].astype(jnp.float32)
        return carry

    lax.fori_loop(0, K, widen, 0, unroll=4)
    out(own, r, 0).start()
    spread(near, one)
    out(one, r + n - 1, 1).start()

    @pl.when(keeps == 0)
    def _():
        spread(far, two)
        out(two, r + 2, 2).start()
        out(two, r + 2, 2).wait()

    out(own, r, 0).wait()
    out(one, r + n - 1, 1).wait()


def place(where, diag, near, far, result):
    K, sub, W = diag.shape
    n = near.shape[0]
    vm = pl.BlockSpec(memory_space=pltpu.VMEM)
    hbm = pl.BlockSpec(memory_space=pltpu.HBM)
    return pl.pallas_call(
        functools.partial(place_kernel, n),
        in_specs=[pl.BlockSpec(memory_space=pltpu.SMEM), vm, vm, vm, hbm],
        out_specs=hbm,
        out_shape=jax.ShapeDtypeStruct((K, sub, n * W), jnp.float32),
        input_output_aliases={4: 0},
        scratch_shapes=[pltpu.VMEM((K, sub, W), jnp.float32)] * 3 + [pltpu.SemaphoreType.DMA((3,))],
        compiler_params=pltpu.CompilerParams(vmem_limit_bytes=40 * 1024 * 1024),
        name="place",
    )(where, diag, near, far, result)


def plan(n):
    homes = {}
    for r in range(n):
        for c in range(n):
            gap = (c - r) % n
            if gap == 1:
                homes[r, c] = (r, 0, 0)
            elif gap == 3:
                homes[r, c] = (c, 1, 2)
            elif gap == 2:
                owner = 0 if 0 in (r, c) else 3
                homes[r, c] = (owner, int(r != owner), 1 if r == owner else 3)
    return homes


def square(chunks, strips, recs):
    n = lax.axis_size("rows")
    axes = ("rows", "cols")
    r, s = lax.axis_index("rows"), lax.axis_index("cols")
    sub = strips[0].shape[1]
    tile, *_ = lax.optimization_barrier((jnp.concatenate(chunks, axis=1), *strips))
    own = own_pairs(tile)
    diag = None
    for k in range(n):
        strip = lax.dynamic_slice_in_dim(own, lax.rem(r + k, n) * sub, sub, 1)
        if k == 0:
            diag = jnp.where(s == r, strip, jnp.zeros_like(strip))
        else:
            diag = diag + lax.ppermute(strip, axes, [(i * n + i, i * n + (i + k) % n) for i in range(n)])
    keeps = jnp.where((r == 0) | (r == n - 1), 1, 0)
    where = jnp.stack([r, s, keeps]).astype(jnp.int32)
    result, msg = pairs(where, recs)
    near, far = [], []
    for k in range(n):
        t = lax.rem(s + k, n)
        for half, kept, moves in ((lax.rem(s, 2), near, [(i, (i + 1) % n) for i in range(n)]), (1 - lax.rem(s, 2), far, [(0, 2), (3, 1)])):
            payload = lax.dynamic_slice(msg, (half, t, 0, 0, 0), (1, 1) + msg.shape[2:])[0, 0]
            perm = [(i * n + j, o * n + (j + k) % n) for i, o in moves for j in range(n)]
            kept.append(lax.ppermute(payload, axes, perm))
    return place(where, diag, jnp.stack(near), jnp.stack(far), result)[None]


def solution(mesh):
    in_specs = (P("crops", None, "rows", "cols"), P(), P(), P(), P(), P(), P())
    out_specs = P("crops", None, ("rows", "cols"), None)

    body = jax.shard_map(shards, mesh=mesh, in_specs=in_specs, out_specs=out_specs, check_vma=False)

    def run(*args):
        with jax.sharding.use_abstract_mesh(mesh.abstract_mesh):
            return body(*args)

    return run
```

```python
import functools

import jax
import jax.numpy as jnp
from jax import lax
from jax.experimental.layout import Layout, with_layout_constraint
from jax.experimental import pallas as pl
from jax.experimental.pallas import tpu as pltpu
from jax.sharding import PartitionSpec as P


BLOCKS = 2
D1 = 4
D2 = 8
CHUNKS = 2

FAR = 1 << 20
ROWS = 4
LEAD = 16


def chain_kernel(cfg, info_ref, t_ref, f_ref, b_ref, e_ref, wa_ref, ba_ref, wb_ref, bb_ref, wo_ref, bo_ref, o_ref, buf, side, sems, X, I, bias, acc, xa, xb):
    H, W, C, whole = cfg
    R = ROWS
    S = W + e_ref.shape[2]
    halo = BLOCKS * (D1 + D2)
    NB = R * S
    T = 256
    BF, F32 = jnp.bfloat16, jnp.float32
    start = info_ref[4]

    def moved(source, a, b, length, q):
        return pltpu.make_async_copy(source.at[pl.ds(a, length)], buf.at[pl.ds(b, length)], sems.at[q])

    middle = moved(f_ref, start, halo, H, 0)
    middle.start()
    sides = pltpu.make_async_copy(e_ref.at[pl.ds(start, H + 2 * halo)], side, sems.at[3])
    sides.start()
    for q, edge_ref, outer, a, b in ((1, t_ref, start == 0, start - halo, 0), (2, b_ref, start + H == whole, start + H, H + halo)):

        @pl.when(outer)
        def _(q=q, edge_ref=edge_ref, b=b):
            moved(edge_ref, 0, b, halo, q).start()

        @pl.when(jnp.logical_not(outer))
        def _(q=q, a=a, b=b):
            moved(f_ref, a, b, halo, q).start()

    def at(row):
        return pl.multiple_of(128 + (row + halo + LEAD) * S, 128)

    for k in range(BLOCKS):
        bias[2 * k] = jnp.broadcast_to(ba_ref[k], (C, 128))
        bias[2 * k + 1] = jnp.broadcast_to(bb_ref[k], (C, 128))
    middle.wait()
    sides.wait()
    moved(t_ref, 0, 0, halo, 1).wait()
    moved(b_ref, 0, H + halo, halo, 2).wait()

    def fill(i, _):
        parts = []
        for q in range(R):
            e = side[i * R + q]
            parts += [e[:, :halo], buf[i * R + q], e[:, halo:]]
        X[:, pl.ds(at(i * R - halo), NB)] = jnp.concatenate(parts, axis=1)
        return 0

    lax.fori_loop(0, (H + 2 * halo) // R, fill, 0)
    lane = lax.broadcasted_iota(jnp.int32, (8, NB), 1)
    col = lane % S
    dead = ((col < halo) & (info_ref[2] > 0)) | ((col >= halo + W) & (info_ref[3] > 0))
    rl = jnp.where(dead, 4 * FAR, lane // S)
    first = jnp.where(info_ref[0] > 0, -start, -FAR)
    last = jnp.where(info_ref[1] > 0, whole - start, FAR)

    def masked(v, row, t):
        p = rl[:, t:t + T]
        m = (p >= first - row) & (p < last - row)
        return jnp.where(m[None], v.reshape(C // 8, 8, T), 0.0).reshape(C, T)

    def biased(v, i):
        b = bias[i]
        return v + jnp.concatenate([b] * (T // 128), axis=1)

    def conv(src, d, w_ref, k, spare, emit):
        n = d // R
        ring = 2 * n + 1
        odd = H // R % 2
        lo = -spare - odd * R
        total = (H + 2 * spare) // R + odd + 2 * n

        def slot(j):
            return pl.multiple_of(lax.rem(j, ring) * NB, 128)

        def shift(j, xs):
            x = src[:, pl.ds(pl.multiple_of(at(lo - d + j * R) - 128, 128), NB + 256)]
            xs[0:C, :] = pltpu.roll(x, d, 1)[:, 128:128 + NB]
            xs[C:2 * C, :] = pltpu.roll(x, NB + 256 - d, 1)[:, 128:128 + NB]

        def step(j, xs, nxt):
            shift(j + 1, nxt)
            row = lo - d + j * R
            s0, s1, s2 = slot(j), slot(j + ring - n), slot(j + ring - 2 * n)
            for t in range(0, NB, T):
                x = jnp.concatenate([xs[0:C, t:t + T], src[:, pl.ds(at(row) + t, T)], xs[C:2 * C, t:t + T]], axis=0)
                y = jnp.dot(w_ref[k], x, preferred_element_type=F32)
                done = acc[:, pl.ds(s2 + t, T)] + y[2 * C:]
                acc[:, pl.ds(s1 + t, T)] += y[C:2 * C]
                acc[:, pl.ds(s0 + t, T)] = y[:C]
                emit(row - d, t, done)

        shift(0, xa)

        def body(i, _):
            step(2 * i, xa, xb)
            step(2 * i + 1, xb, xa)
            return 0

        lax.fori_loop(0, total // 2, body, 0)

    def block(k, carry):
        edge = (BLOCKS - k) * (D1 + D2)

        def emit_a(row, t, v):
            v = biased(v, 2 * k)
            e = jnp.where(v > 0, v, jnp.exp(v) - 1.0)
            I[:, pl.ds(at(row) + t, T)] = masked(e, row, t).astype(BF)

        conv(X, D1, wa_ref, k, edge - D1, emit_a)

        def emit_b(row, t, v):
            v = biased(v, 2 * k + 1) + X[:, pl.ds(at(row) + t, T)].astype(F32)
            X[:, pl.ds(at(row) + t, T)] = masked(v, row, t).astype(BF)

        conv(I, D2, wb_ref, k, edge - D1 - D2, emit_b)
        return carry

    lax.fori_loop(0, BLOCKS, block, 0)
    bo = jnp.broadcast_to(bo_ref[...], (bo_ref.shape[0], W))

    def project(i, _):
        x = X[:, pl.ds(at(i * R), NB)]
        for q in range(R):
            g = jnp.dot(wo_ref[...], x[:, q * S + halo:q * S + halo + W], preferred_element_type=F32) + bo
            o_ref[i * R + q] = g.astype(BF)
        return 0

    lax.fori_loop(0, H // R, project, 0)


def chain(info, top, field, bottom, side, wa, ba, wb, bb, wo, bo, H):
    whole, C, W = field.shape
    S = W + side.shape[2]
    K = wo.shape[0]
    R = ROWS
    halo = BLOCKS * (D1 + D2)
    N = 128 + (H + 2 * halo + LEAD + R) * S + 256
    KP = -(-K // 16) * 16
    wo = jnp.pad(wo, ((0, KP - K), (0, 0)))
    bo = jnp.pad(bo, (0, KP - K))[:, None]
    vm = pl.BlockSpec(memory_space=pltpu.VMEM)
    ring = (2 * (max(D1, D2) // R) + 1) * R * S
    flops = 2 * BLOCKS * 2 * 9 * C * C * H * S
    out = pl.pallas_call(
        functools.partial(chain_kernel, (H, W, C, whole)),
        out_shape=jax.ShapeDtypeStruct((H, KP, W), jnp.bfloat16),
        in_specs=[pl.BlockSpec(memory_space=pltpu.SMEM), *[pl.BlockSpec(memory_space=pltpu.HBM)] * 4] + [vm] * 6,
        out_specs=vm,
        scratch_shapes=[
            pltpu.VMEM((H + 2 * halo, C, W), jnp.bfloat16),
            pltpu.VMEM((H + 2 * halo, C, S - W), jnp.bfloat16),
            pltpu.SemaphoreType.DMA((4,)),
            pltpu.VMEM((C, N), jnp.bfloat16),
            pltpu.VMEM((C, N), jnp.bfloat16),
            pltpu.VMEM((2 * BLOCKS, C, 128), jnp.float32),
            pltpu.VMEM((C, ring), jnp.float32),
            pltpu.VMEM((2 * C, R * S), jnp.bfloat16),
            pltpu.VMEM((2 * C, R * S), jnp.bfloat16),
        ],
        compiler_params=pltpu.CompilerParams(vmem_limit_bytes=63000 * 1024),
        cost_estimate=pl.CostEstimate(flops=flops, bytes_accessed=4 * C * H * S, transcendentals=2 * C * H * S),
        name="chain",
    )(info, top, field, bottom, side, wa, ba[:, :, None], wb, bb[:, :, None], wo, bo)
    return out[:, :K]


def neighbours(first, last, axis):
    peers = lax.axis_size(axis)
    up = [(i, i + 1) for i in range(peers - 1)]
    down = [(j, i) for i, j in up]
    return lax.ppermute(last, axis, up), lax.ppermute(first, axis, down)


def rims(tile):
    halo = BLOCKS * (D1 + D2)
    W = tile.shape[2]
    above, below = neighbours(tile[:, :halo], tile[:, -halo:], "rows")
    lane = jnp.arange(2 * halo)
    pick = jnp.where(lane < halo, lane, W - 2 * halo + lane)[:, None] == jnp.arange(W)[None, :]
    ends = jnp.einsum("dq,cpq->cdp", pick.astype(tile.dtype), tile, preferred_element_type=tile.dtype)
    left, right = neighbours(ends[:, :halo], ends[:, halo:], "cols")
    sides = jnp.concatenate([left, right], axis=1)
    up, down = neighbours(sides[:, :, :halo], sides[:, :, -halo:], "rows")
    corners = jnp.stack([up[:, :halo], up[:, halo:], down[:, :halo], down[:, halo:]], axis=1)
    return above, below, left, right, corners


def shards(pair_maps, conv_a, bias_a, conv_b, bias_b, out_weight, out_bias):
    rows, cols = lax.axis_size("rows"), lax.axis_size("cols")
    _, C, H, W = pair_maps.shape
    halo = BLOCKS * (D1 + D2)
    r, c = lax.axis_index("rows"), lax.axis_index("cols")
    edge = jnp.stack([r == 0, r == rows - 1, c == 0, c == cols - 1]).astype(jnp.int32)
    tile = pair_maps[0]
    above, below, left, right, corners = rims(tile)
    flat = jnp.concatenate

    def sides(left, right, corners, second, third):
        west = flat([corners[:, 0], left, corners[:, third]], axis=2)
        east = flat([corners[:, second], right, corners[:, 3]], axis=2)
        return west, east

    def caller(top, field, bottom, west, east, wa, wb, length):
        gap = jnp.zeros((C, 64 - 2 * halo, west.shape[2]), west.dtype)
        west, east, top, bottom = (with_layout_constraint(v, Layout((0, 1, 2))) for v in (west, east, top, bottom))
        side = with_layout_constraint(flat([west, east, gap], axis=1), Layout((0, 1, 2)))
        side, top, bottom = lax.optimization_barrier((side, top, bottom))
        side, top, bottom = jnp.transpose(side, (2, 0, 1)), jnp.transpose(top, (1, 0, 2)), jnp.transpose(bottom, (1, 0, 2))
        return lambda info: chain(info, top, field, bottom, side, wa, bias_a, wb, bias_b, out_weight, out_bias, length)

    square_grid = rows == 4 and cols == 4 and H == W and H // rows == 64

    def merged(w):
        return w.reshape(BLOCKS, 3 * C, 3 * C)

    if square_grid:
        me = r * cols + c
        homes = plan(cols)
        turn, off = (jnp.array([homes.get((i // cols, i % cols), (0, 0, 2 * (2 * i < rows * cols)))[q] for i in range(rows * cols)])[me] for q in (1, 2))
        field = lax.cond(turn > 0, lambda v: jnp.transpose(v, (2, 0, 1)), lambda v: jnp.transpose(v, (1, 0, 2)), tile)
        fixed = with_layout_constraint(jnp.swapaxes(corners, 2, 3), Layout((0, 1, 2, 3)))
        corners = jnp.where(turn > 0, fixed[:, jnp.array([0, 2, 1, 3])], with_layout_constraint(corners, Layout((0, 1, 2, 3))))
        north, south, west, east = (jnp.where(turn > 0, a, b) for a, b in ((left, above), (right, below), (above, left), (below, right)))
        west, east = sides(west, east, corners, 1, 2)
        edge = jnp.where(turn > 0, edge[jnp.array([2, 3, 0, 1])], edge)

        def turned(w):
            other = jnp.transpose(w.reshape(BLOCKS, 3, C, 3, C), (0, 3, 2, 1, 4))
            return jnp.where(turn > 0, merged(other), merged(w))

        wa, wb = turned(conv_a), turned(conv_b)
        q = cols // CHUNKS
        run = caller(north, field, south, west, east, wa, wb, H // CHUNKS)
        chunks, strips, recs = [], [], []
        for j in range(CHUNKS):
            info = jnp.append(edge, ((j * q) ^ (off & ~(q - 1))) * (H // cols))
            if j:
                info, *_ = lax.optimization_barrier((info, *strips[-q:], ahead))
            chunks.append(jnp.transpose(run(info), (1, 0, 2)))
            for m in range(j * q, j * q + q):
                strips.append(lax.dynamic_slice_in_dim(chunks[j], ((m % q) ^ (off & (q - 1))) * (H // cols), H // cols, 1))
                perm = [(i * cols + k, home * cols + (m ^ o)) for (i, k), (home, _, o) in homes.items()]
                recs.append(lax.ppermute(strips[m], ("rows", "cols"), perm))
            if not j:
                ahead = own_pairs(lax.dynamic_slice_in_dim(chunks[0], (off & 2) * (H // cols), W // CHUNKS, 2))
                early = crossing(ahead)
        return square(chunks, strips, recs, early, off)
    field = jnp.transpose(tile, (1, 0, 2))
    west, east = sides(left, right, corners, 1, 2)
    logits = caller(above, field, below, west, east, merged(conv_a), merged(conv_b), H)(jnp.append(edge, 0))
    logits = jnp.transpose(logits, (1, 0, 2))[None]
    strips = lax.all_to_all(logits, "cols", split_axis=2, concat_axis=3, tiled=True)
    flipped = lax.all_to_all(strips, ("rows", "cols"), split_axis=3, concat_axis=2, tiled=True)
    mirrored = jnp.swapaxes(flipped, 2, 3)
    symmetric = (strips.astype(jnp.float32) + mirrored.astype(jnp.float32)) * 0.5
    return symmetric - jnp.log(jnp.sum(jnp.exp(symmetric), axis=1, keepdims=True))


def pair_kernel(n, where_ref, r0, r1, r2, r3, o_ref, msg, lab, sems):
    K, sub, lanes = r0.shape
    r, s, keeps = where_ref[0], where_ref[1], where_ref[2]
    g = pl.program_id(0)
    W = lanes * pl.num_programs(0)

    def out(p, tile):
        spot = pl.multiple_of(lax.rem(tile, n) * W + g * lanes, lanes)
        return pltpu.make_async_copy(lab.at[p], o_ref.at[:, :, pl.ds(spot, lanes)], sems.at[p])

    for p, (one, two) in enumerate(((r0, r2), (r1, r3))):
        total = jnp.zeros((sub, lanes), jnp.float32)
        for k in range(K):
            v = (one[k].astype(jnp.float32) + two[k].astype(jnp.float32)) * 0.5
            lab[p, k] = v
            total = total + jnp.exp(v)
        norm = jnp.log(total)
        for k in range(K):
            v = lab[p, k] - norm
            lab[p, k] = v
            w = v.T
            for t in range(lanes // sub):
                b = w[t * sub:(t + 1) * sub]
                msg[p, t, k] = jnp.concatenate([b[:sub // 2], b[sub // 2:]], axis=1).astype(jnp.bfloat16)

        @pl.when(lax.rem(s, 2) == p)
        def _(p=p):
            out(p, r + 1).start()

        @pl.when((lax.rem(s, 2) != p) & (keeps > 0))
        def _(p=p):
            out(p, r + 2).start()

    for p in range(2):

        @pl.when((lax.rem(s, 2) == p) | (keeps > 0))
        def _(p=p):
            out(p, 0).wait()


def pairs(where, recs):
    K, sub, W = recs[0].shape
    lanes, n = 128, len(recs)
    return pl.pallas_call(
        functools.partial(pair_kernel, n),
        grid=(W // lanes,),
        in_specs=[pl.BlockSpec(memory_space=pltpu.SMEM)] + [pl.BlockSpec((K, sub, lanes), lambda i: (0, 0, i))] * 4,
        out_specs=[
            pl.BlockSpec(memory_space=pltpu.HBM),
            pl.BlockSpec((2, lanes // sub, K, sub // 2, 2 * sub), lambda i: (0, i, 0, 0, 0)),
        ],
        out_shape=[
            jax.ShapeDtypeStruct((K, sub, n * W), jnp.float32),
            jax.ShapeDtypeStruct((2, W // sub, K, sub // 2, 2 * sub), jnp.bfloat16),
        ],
        scratch_shapes=[pltpu.VMEM((2, K, sub, lanes), jnp.float32), pltpu.SemaphoreType.DMA((2,))],
        name="pairs",
    )(where, *recs)


def own_kernel(a_ref, b_ref, o_ref, tmp):
    K = a_ref.shape[0]

    def add(k, total):
        v = (a_ref[k].astype(jnp.float32) + b_ref[k].astype(jnp.float32).T) * 0.5
        tmp[k] = v
        return total + jnp.exp(v)

    norm = jnp.log(lax.fori_loop(0, K, add, jnp.zeros(tmp.shape[1:], jnp.float32), unroll=2))

    def emit(k, carry):
        o_ref[k] = (tmp[k] - norm).astype(jnp.bfloat16)
        return carry

    lax.fori_loop(0, K, emit, 0, unroll=2)


def own_pairs(tile):
    K, H, W = tile.shape
    B = 128
    return pl.pallas_call(
        own_kernel,
        grid=(H // B, W // B),
        in_specs=[pl.BlockSpec((K, B, B), lambda i, j: (0, i, j)), pl.BlockSpec((K, B, B), lambda i, j: (0, j, i))],
        out_specs=pl.BlockSpec((K, B, B), lambda i, j: (0, i, j)),
        out_shape=jax.ShapeDtypeStruct((K, H, W), jnp.bfloat16),
        scratch_shapes=[pltpu.VMEM((K, B, B), jnp.float32)],
        cost_estimate=pl.CostEstimate(flops=6 * K * H * W, bytes_accessed=6 * K * H * W, transcendentals=K * H * W),
        name="own",
    )(tile, tile)


def place_kernel(n, where_ref, mine, other, e0, e1, l0, l1, near, far, _, o_ref, own, one, two, sems):
    K, sub, W = mine.shape
    F32 = jnp.float32
    r, s, keeps = where_ref[0], where_ref[1], where_ref[2]

    def out(source, tile, q):
        spot = pl.multiple_of(lax.rem(tile, n) * W, W)
        return pltpu.make_async_copy(source, o_ref.at[:, :, pl.ds(spot, W)], sems.at[q])

    def spread(source, target):
        def body(k, carry):
            pieces = []
            for b in range(n):
                v = source[lax.rem(s + n - b, n), k].astype(jnp.float32)
                pieces.append(jnp.concatenate([v[:, :sub], v[:, sub:]], axis=0))
            target[k] = jnp.concatenate(pieces, axis=1)
            return carry

        lax.fori_loop(0, K, body, 0, unroll=4)

    def each(fn):
        def body(k, carry):
            own[k] = fn(k)
            return carry

        lax.fori_loop(0, K, body, 0, unroll=4)

    def both(a, b, k):
        return a[k].astype(F32) + b[k].astype(F32)

    beside = r + 1 - 2 * lax.rem(r, 2)

    @pl.when(s == r)
    def _():
        each(lambda k: mine[k].astype(F32))

    @pl.when(s == beside)
    def _():
        each(lambda k: other[k].astype(F32))

    @pl.when((s != r) & (s != beside) & (2 * r < n))
    def _():
        each(lambda k: jnp.concatenate([both(l0, l1, k), both(e0, e1, k)], axis=1))

    @pl.when((s != r) & (s != beside) & (2 * r >= n))
    def _():
        each(lambda k: jnp.concatenate([both(e0, e1, k), both(l0, l1, k)], axis=1))

    out(own, r, 0).start()
    spread(near, one)
    out(one, r + n - 1, 1).start()

    @pl.when(keeps == 0)
    def _():
        spread(far, two)
        out(two, r + 2, 2).start()
        out(two, r + 2, 2).wait()

    out(own, r, 0).wait()
    out(one, r + n - 1, 1).wait()


def place(where, diag, near, far, result):
    K, sub, W = diag[0].shape
    n = near.shape[0]
    vm = pl.BlockSpec(memory_space=pltpu.VMEM)
    hbm = pl.BlockSpec(memory_space=pltpu.HBM)
    return pl.pallas_call(
        functools.partial(place_kernel, n),
        in_specs=[pl.BlockSpec(memory_space=pltpu.SMEM), *[vm] * (len(diag) + 2), hbm],
        out_specs=hbm,
        out_shape=jax.ShapeDtypeStruct((K, sub, n * W), jnp.float32),
        input_output_aliases={len(diag) + 3: 0},
        scratch_shapes=[pltpu.VMEM((K, sub, W), jnp.float32)] * 3 + [pltpu.SemaphoreType.DMA((3,))],
        compiler_params=pltpu.CompilerParams(vmem_limit_bytes=40 * 1024 * 1024),
        name="place",
    )(where, *diag, near, far, result)


def plan(n):
    homes = {}
    for r in range(n):
        for c in range(n):
            gap = (c - r) % n
            if gap == 1:
                homes[r, c] = (r, 0, 0)
            elif gap == 3:
                homes[r, c] = (c, 1, 2)
            elif gap == 2:
                owner = 0 if 0 in (r, c) else 3
                homes[r, c] = (owner, int(r != owner), 1 if r == owner else 3)
    return homes


def crossing(block):
    n = lax.axis_size("rows")
    sub = block.shape[1] // (n // 2)
    got = []
    for e in range(n // 2):
        perm = [(i * n + i, i * n + (n // 2 if 2 * i < n else 0) + e) for i in range(n)]
        got.append(lax.ppermute(block[:, e * sub:(e + 1) * sub], ("rows", "cols"), perm))
    return got


def rest_kernel(h_ref, a_ref, b_ref, c_ref, near_ref, far_ref, tmp):
    K = a_ref.shape[0]
    first = pl.program_id(0) == 0

    def add(k, total):
        other = jnp.where(first, b_ref[k].astype(jnp.float32), c_ref[k].astype(jnp.float32))
        v = (a_ref[k].astype(jnp.float32) + other.T) * 0.5
        tmp[k] = v
        return total + jnp.exp(v)

    norm = jnp.log(lax.fori_loop(0, K, add, jnp.zeros(tmp.shape[1:], jnp.float32), unroll=2))

    def emit(k, carry):
        v = tmp[k] - norm
        near_ref[k] = v.astype(jnp.bfloat16)
        far_ref[k] = v.T.astype(jnp.bfloat16)
        return carry

    lax.fori_loop(0, K, emit, 0, unroll=2)


def rest_pairs(half, far_rows, near_rows):
    K, B, W = near_rows.shape
    return pl.pallas_call(
        rest_kernel,
        grid_spec=pltpu.PrefetchScalarGridSpec(
            num_scalar_prefetch=1,
            grid=(2,),
            in_specs=[
                pl.BlockSpec((K, B, B), lambda g, h: (0, 0, (1 - h[0]) * (1 - g) + h[0] * g)),
                pl.BlockSpec((K, B, B), lambda g, h: (0, 0, 1 - h[0])),
                pl.BlockSpec((K, B, B), lambda g, h: (0, 0, 1 - h[0])),
            ],
            out_specs=[
                pl.BlockSpec((K, B, B), lambda g, h: (0, 0, (1 - h[0]) * (1 - g) + h[0] * g)),
                pl.BlockSpec((K, B, B), lambda g, h: (0, 0, 0)),
            ],
            scratch_shapes=[pltpu.VMEM((K, B, B), jnp.float32)],
        ),
        out_shape=[jax.ShapeDtypeStruct((K, B, W), jnp.bfloat16), jax.ShapeDtypeStruct((K, B, B), jnp.bfloat16)],
        cost_estimate=pl.CostEstimate(flops=6 * K * B * W, bytes_accessed=6 * K * B * W, transcendentals=K * B * W),
        name="rest",
    )(half, near_rows, near_rows, far_rows)


def square(chunks, strips, recs, early, off):
    n = lax.axis_size("rows")
    axes = ("rows", "cols")
    r, s = lax.axis_index("rows"), lax.axis_index("cols")
    sub = strips[0].shape[1]
    far_rows, near_rows, *_ = lax.optimization_barrier((*chunks, *strips))
    near, far = rest_pairs((off // 2)[None].astype(jnp.int32), far_rows, near_rows)
    late = crossing(far)
    mine, other = (lax.dynamic_slice_in_dim(near, v * sub, sub, 1) for v in (r % 2, 1 - r % 2))
    other = lax.ppermute(other, axes, [(i * n + i, i * n + (i ^ 1)) for i in range(n)])
    keeps = jnp.where((r == 0) | (r == n - 1), 1, 0)
    where = jnp.stack([r, s, keeps]).astype(jnp.int32)
    result, msg = pairs(where, recs)
    near, far = [], []
    for k in range(n):
        t = lax.rem(s + k, n)
        for half, kept, moves in ((lax.rem(s, 2), near, [(i, (i + 1) % n) for i in range(n)]), (1 - lax.rem(s, 2), far, [(0, 2), (3, 1)])):
            payload = lax.dynamic_slice(msg, (half, t, 0, 0, 0), (1, 1) + msg.shape[2:])[0, 0]
            perm = [(i * n + j, o * n + (j + k) % n) for i, o in moves for j in range(n)]
            kept.append(lax.ppermute(payload, axes, perm))
    return place(where, [mine, other, *early, *late], jnp.stack(near), jnp.stack(far), result)[None]


def solution(mesh):
    in_specs = (P("crops", None, "rows", "cols"), P(), P(), P(), P(), P(), P())
    out_specs = P("crops", None, ("rows", "cols"), None)

    body = jax.shard_map(shards, mesh=mesh, in_specs=in_specs, out_specs=out_specs, check_vma=False)

    def run(*args):
        with jax.sharding.use_abstract_mesh(mesh.abstract_mesh):
            return body(*args)

    return run
```

```python
import functools

import jax
import jax.numpy as jnp
import numpy as np
from jax import lax
from jax.experimental.layout import Layout, with_layout_constraint
from jax.experimental import pallas as pl
from jax.experimental.pallas import tpu as pltpu
from jax.sharding import PartitionSpec as P


BLOCKS = 2
D1 = 4
D2 = 8
CHUNKS = 2

FAR = 1 << 20
ROWS = 4
LEAD = 16
KEEPS, TURN, ORDER, HALF, EDGE, FIRST = 2, 3, 4, 5, 6, 10


def chain_kernel(cfg, info_ref, t_ref, f_ref, b_ref, e_ref, ra_ref, rb_ref, wo_ref, add_ref, o_ref, buf, side, sems, X, I, bias, acc, xa, xb, wa_ref, wb_ref):
    H, W, C, whole, chunk = cfg
    R = ROWS
    S = W + e_ref.shape[2]
    halo = BLOCKS * (D1 + D2)
    NB = R * S
    T = 256
    BF, F32 = jnp.bfloat16, jnp.float32
    start = pl.multiple_of(info_ref[FIRST + chunk], ROWS)

    def moved(source, a, b, length, q):
        return pltpu.make_async_copy(source.at[pl.ds(a, length)], buf.at[pl.ds(b, length)], sems.at[q])

    middle = moved(f_ref, start, halo, H, 0)
    middle.start()
    sides = pltpu.make_async_copy(e_ref.at[pl.ds(start, H + 2 * halo)], side, sems.at[3])
    sides.start()
    for q, edge_ref, outer, a, b in ((1, t_ref, start == 0, start - halo, 0), (2, b_ref, start + H == whole, start + H, H + halo)):

        @pl.when(outer)
        def _(q=q, edge_ref=edge_ref, b=b):
            moved(edge_ref, 0, b, halo, q).start()

        @pl.when(jnp.logical_not(outer))
        def _(q=q, a=a, b=b):
            moved(f_ref, a, b, halo, q).start()

    def at(row):
        return pl.multiple_of(128 + (row + halo + LEAD) * S, 128)

    for k in range(2 * BLOCKS):
        bias[k] = jnp.broadcast_to(add_ref[:, k:k + 1], (C, 128))

    def weights(turned):
        for raw, w in ((ra_ref, wa_ref), (rb_ref, wb_ref)):
            for k in range(BLOCKS):
                for a in range(3):
                    for b in range(3):
                        p, q = (b, a) if turned else (a, b)
                        w[k, p * C:(p + 1) * C, q * C:(q + 1) * C] = raw[k, a, :, b * C:(b + 1) * C]

    @pl.when(info_ref[TURN] > 0)
    def _():
        weights(True)

    @pl.when(info_ref[TURN] == 0)
    def _():
        weights(False)

    middle.wait()
    sides.wait()
    moved(t_ref, 0, 0, halo, 1).wait()
    moved(b_ref, 0, H + halo, halo, 2).wait()

    def fill(i, _):
        parts = []
        for q in range(R):
            e = side[i * R + q]
            parts += [e[:, :halo], buf[i * R + q], e[:, halo:]]
        X[:, pl.ds(at(i * R - halo), NB)] = jnp.concatenate(parts, axis=1)
        return 0

    lax.fori_loop(0, (H + 2 * halo) // R, fill, 0)
    lane = lax.broadcasted_iota(jnp.int32, (8, NB), 1)
    col = lane % S
    dead = ((col < halo) & (info_ref[EDGE + 2] > 0)) | ((col >= halo + W) & (info_ref[EDGE + 3] > 0))
    rl = jnp.where(dead, 4 * FAR, lane // S)
    first = jnp.where(info_ref[EDGE] > 0, -start, -FAR)
    last = jnp.where(info_ref[EDGE + 1] > 0, whole - start, FAR)

    def masked(v, row, t):
        p = rl[:, t:t + T]
        m = (p >= first - row) & (p < last - row)
        return jnp.where(m[None], v.reshape(C // 8, 8, T), 0.0).reshape(C, T)

    def biased(v, i):
        b = bias[i]
        return v + jnp.concatenate([b] * (T // 128), axis=1)

    def conv(src, d, w_ref, k, spare, emit):
        n = d // R
        ring = 2 * n + 1
        odd = H // R % 2
        lo = -spare - odd * R
        total = (H + 2 * spare) // R + odd + 2 * n

        def slot(j):
            return pl.multiple_of(lax.rem(j, ring) * NB, 128)

        def shift(j, xs):
            x = src[:, pl.ds(pl.multiple_of(at(lo - d + j * R) - 128, 128), NB + 256)]
            xs[0:C, :] = pltpu.roll(x, d, 1)[:, 128:128 + NB]
            xs[C:2 * C, :] = pltpu.roll(x, NB + 256 - d, 1)[:, 128:128 + NB]

        def step(j, xs, nxt):
            shift(j + 1, nxt)
            row = lo - d + j * R
            s0, s1, s2 = slot(j), slot(j + ring - n), slot(j + ring - 2 * n)
            for t in range(0, NB, T):
                x = jnp.concatenate([xs[0:C, t:t + T], src[:, pl.ds(at(row) + t, T)], xs[C:2 * C, t:t + T]], axis=0)
                y = jnp.dot(w_ref[k], x, preferred_element_type=F32)
                done = acc[:, pl.ds(s2 + t, T)] + y[2 * C:]
                acc[:, pl.ds(s1 + t, T)] += y[C:2 * C]
                acc[:, pl.ds(s0 + t, T)] = y[:C]
                emit(row - d, t, done)

        shift(0, xa)

        def body(i, _):
            step(2 * i, xa, xb)
            step(2 * i + 1, xb, xa)
            return 0

        lax.fori_loop(0, total // 2, body, 0)

    def block(k, carry):
        edge = (BLOCKS - k) * (D1 + D2)

        def emit_a(row, t, v):
            v = biased(v, k)
            e = jnp.where(v > 0, v, jnp.exp(v) - 1.0)
            I[:, pl.ds(at(row) + t, T)] = masked(e, row, t).astype(BF)

        conv(X, D1, wa_ref, k, edge - D1, emit_a)

        def emit_b(row, t, v):
            v = biased(v, BLOCKS + k) + X[:, pl.ds(at(row) + t, T)].astype(F32)
            X[:, pl.ds(at(row) + t, T)] = masked(v, row, t).astype(BF)

        conv(I, D2, wb_ref, k, edge - D1 - D2, emit_b)
        return carry

    lax.fori_loop(0, BLOCKS, block, 0)
    K = wo_ref.shape[0]
    bo = jnp.broadcast_to(add_ref[:K, 2 * BLOCKS:2 * BLOCKS + 1], (K, W))

    def project(i, _):
        x = X[:, pl.ds(at(i * R), NB)]
        for q in range(R):
            g = jnp.dot(wo_ref[...], x[:, q * S + halo:q * S + halo + W], preferred_element_type=F32) + bo
            o_ref[i * R + q] = g.astype(BF)
        return 0

    lax.fori_loop(0, H // R, project, 0)


def chain(info, chunk, top, field, bottom, side, wa, wb, wo, add, H):
    whole, C, W = field.shape
    S = W + side.shape[2]
    K = wo.shape[0]
    R = ROWS
    halo = BLOCKS * (D1 + D2)
    N = 128 + (H + 2 * halo + LEAD + R) * S + 256
    vm = pl.BlockSpec(memory_space=pltpu.VMEM)
    ring = (2 * (max(D1, D2) // R) + 1) * R * S
    flops = 2 * BLOCKS * 2 * 9 * C * C * H * S
    return pl.pallas_call(
        functools.partial(chain_kernel, (H, W, C, whole, chunk)),
        out_shape=jax.ShapeDtypeStruct((H, K, W), jnp.bfloat16),
        in_specs=[pl.BlockSpec(memory_space=pltpu.SMEM), *[pl.BlockSpec(memory_space=pltpu.HBM)] * 4] + [vm] * 4,
        out_specs=vm,
        scratch_shapes=[
            pltpu.VMEM((H + 2 * halo, C, W), jnp.bfloat16),
            pltpu.VMEM((H + 2 * halo, C, S - W), jnp.bfloat16),
            pltpu.SemaphoreType.DMA((4,)),
            pltpu.VMEM((C, N), jnp.bfloat16),
            pltpu.VMEM((C, N), jnp.bfloat16),
            pltpu.VMEM((2 * BLOCKS, C, 128), jnp.float32),
            pltpu.VMEM((C, ring), jnp.float32),
            pltpu.VMEM((2 * C, R * S), jnp.bfloat16),
            pltpu.VMEM((2 * C, R * S), jnp.bfloat16),
            pltpu.VMEM((BLOCKS, 3 * C, 3 * C), jnp.bfloat16),
            pltpu.VMEM((BLOCKS, 3 * C, 3 * C), jnp.bfloat16),
        ],
        compiler_params=pltpu.CompilerParams(vmem_limit_bytes=63000 * 1024),
        cost_estimate=pl.CostEstimate(flops=flops, bytes_accessed=4 * C * H * S, transcendentals=2 * C * H * S),
        name="chain",
    )(info, top, field, bottom, side, wa, wb, wo, add)


def neighbours(first, last, axis):
    peers = lax.axis_size(axis)
    up = [(i, i + 1) for i in range(peers - 1)]
    down = [(j, i) for i, j in up]
    return lax.ppermute(last, axis, up), lax.ppermute(first, axis, down)


def rims(tile):
    halo = BLOCKS * (D1 + D2)
    W = tile.shape[2]
    above, below = neighbours(tile[:, :halo], tile[:, -halo:], "rows")
    lane = jnp.arange(2 * halo)
    pick = jnp.where(lane < halo, lane, W - 2 * halo + lane)[:, None] == jnp.arange(W)[None, :]
    ends = jnp.einsum("dq,cpq->cdp", pick.astype(tile.dtype), tile, preferred_element_type=tile.dtype)
    left, right = neighbours(ends[:, :halo], ends[:, halo:], "cols")
    sides = jnp.concatenate([left, right], axis=1)
    up, down = neighbours(sides[:, :, :halo], sides[:, :, -halo:], "rows")
    corners = jnp.stack([up[:, :halo], up[:, halo:], down[:, :halo], down[:, halo:]], axis=1)
    return above, below, left, right, corners


def table(rows, cols, homes, step):
    lines = []
    for r in range(rows):
        for c in range(cols):
            diagonal = 2 * (2 * r < rows) if homes else 0
            _, turn, order = homes.get((r, c), (0, 0, diagonal))
            edge = [r == 0, r == rows - 1, c == 0, c == cols - 1]
            if turn:
                edge = edge[2:] + edge[:2]
            chunks = CHUNKS if homes else 1
            q = cols // chunks
            starts = [((j * q) ^ (order & ~(q - 1))) * step if homes else 0 for j in range(chunks)]
            lines.append([r, c, r in (0, rows - 1), turn, order, order // 2, *edge, *starts])
    return np.array(lines, np.int32)


def shards(pair_maps, conv_a, bias_a, conv_b, bias_b, out_weight, out_bias):
    rows, cols = lax.axis_size("rows"), lax.axis_size("cols")
    _, C, H, W = pair_maps.shape
    K = out_bias.shape[0]
    halo = BLOCKS * (D1 + D2)
    me = lax.axis_index("rows") * cols + lax.axis_index("cols")
    square_grid = rows == 4 and cols == 4 and H == W and H // rows == 64
    homes = plan(cols) if square_grid else {}
    lines = table(rows, cols, homes, H // cols)
    info = lax.dynamic_slice(jnp.asarray(lines), (me, 0), (1, lines.shape[1]))[0]
    add = jnp.concatenate([bias_a.T, bias_b.T, jnp.pad(out_bias, (0, C - K))[:, None]], axis=1)
    tile = pair_maps[0]
    turn, off = info[TURN], info[ORDER]

    def upright(v):
        return jnp.transpose(v, (1, 0, 2))

    field = lax.cond(turn > 0, lambda v: jnp.transpose(v, (2, 0, 1)), upright, tile) if square_grid else upright(tile)
    above, below, left, right, corners = rims(tile)
    flat = jnp.concatenate

    def sides(left, right, corners, second, third):
        west = flat([corners[:, 0], left, corners[:, third]], axis=2)
        east = flat([corners[:, second], right, corners[:, 3]], axis=2)
        return west, east

    def caller(top, bottom, west, east, length):
        gap = jnp.zeros((C, 64 - 2 * halo, west.shape[2]), west.dtype)
        west, east, top, bottom = (with_layout_constraint(v, Layout((0, 1, 2))) for v in (west, east, top, bottom))
        side = with_layout_constraint(flat([west, east, gap], axis=1), Layout((0, 1, 2)))
        side, top, bottom = lax.optimization_barrier((side, top, bottom))
        side, top, bottom = jnp.transpose(side, (2, 0, 1)), jnp.transpose(top, (1, 0, 2)), jnp.transpose(bottom, (1, 0, 2))
        return lambda info, j: chain(info, j, top, field, bottom, side, conv_a, conv_b, out_weight, add, length)

    square_grid = rows == 4 and cols == 4 and H == W and H // rows == 64

    if square_grid:
        fixed = with_layout_constraint(jnp.swapaxes(corners, 2, 3), Layout((0, 1, 2, 3)))
        corners = jnp.where(turn > 0, fixed[:, jnp.array([0, 2, 1, 3])], with_layout_constraint(corners, Layout((0, 1, 2, 3))))
        north, south, west, east = (jnp.where(turn > 0, a, b) for a, b in ((left, above), (right, below), (above, left), (below, right)))
        west, east = sides(west, east, corners, 1, 2)
        q = cols // CHUNKS
        run = caller(north, south, west, east, H // CHUNKS)
        chunks, strips, recs = [], [], []
        for j in range(CHUNKS):
            place_of = info
            if j:
                place_of, *_ = lax.optimization_barrier((info, *strips[-q:], ahead))
            chunks.append(upright(run(place_of, j)))
            for m in range(j * q, j * q + q):
                strips.append(lax.dynamic_slice_in_dim(chunks[j], ((m % q) ^ (off & (q - 1))) * (H // cols), H // cols, 1))
                perm = [(i * cols + k, home * cols + (m ^ o)) for (i, k), (home, _, o) in homes.items()]
                recs.append(lax.ppermute(strips[m], ("rows", "cols"), perm))
            if not j:
                ahead = own_pairs(lax.dynamic_slice_in_dim(chunks[0], (off & 2) * (H // cols), W // CHUNKS, 2))
                early = crossing(ahead)
        return square(chunks, strips, recs, early, info)
    west, east = sides(left, right, corners, 1, 2)
    logits = caller(above, below, west, east, H)(info, 0)
    logits = jnp.transpose(logits, (1, 0, 2))[None]
    strips = lax.all_to_all(logits, "cols", split_axis=2, concat_axis=3, tiled=True)
    flipped = lax.all_to_all(strips, ("rows", "cols"), split_axis=3, concat_axis=2, tiled=True)
    mirrored = jnp.swapaxes(flipped, 2, 3)
    symmetric = (strips.astype(jnp.float32) + mirrored.astype(jnp.float32)) * 0.5
    return symmetric - jnp.log(jnp.sum(jnp.exp(symmetric), axis=1, keepdims=True))


def pair_kernel(n, where_ref, r0, r1, r2, r3, o_ref, msg, lab, sems):
    K, sub, lanes = r0.shape
    r, s, keeps = where_ref[0], where_ref[1], where_ref[KEEPS]
    g = pl.program_id(0)
    W = lanes * pl.num_programs(0)

    def out(p, tile):
        spot = pl.multiple_of(lax.rem(tile, n) * W + g * lanes, lanes)
        return pltpu.make_async_copy(lab.at[p], o_ref.at[:, :, pl.ds(spot, lanes)], sems.at[p])

    for p, (one, two) in enumerate(((r0, r2), (r1, r3))):
        total = jnp.zeros((sub, lanes), jnp.float32)
        for k in range(K):
            v = (one[k].astype(jnp.float32) + two[k].astype(jnp.float32)) * 0.5
            lab[p, k] = v
            total = total + jnp.exp(v)
        norm = jnp.log(total)
        for k in range(K):
            v = lab[p, k] - norm
            lab[p, k] = v
            w = v.T
            for t in range(lanes // sub):
                b = w[t * sub:(t + 1) * sub]
                msg[p, t, k] = jnp.concatenate([b[:sub // 2], b[sub // 2:]], axis=1).astype(jnp.bfloat16)

        @pl.when(lax.rem(s, 2) == p)
        def _(p=p):
            out(p, r + 1).start()

        @pl.when((lax.rem(s, 2) != p) & (keeps > 0))
        def _(p=p):
            out(p, r + 2).start()

    for p in range(2):

        @pl.when((lax.rem(s, 2) == p) | (keeps > 0))
        def _(p=p):
            out(p, 0).wait()


def pairs(where, recs):
    K, sub, W = recs[0].shape
    lanes, n = 128, len(recs)
    return pl.pallas_call(
        functools.partial(pair_kernel, n),
        grid=(W // lanes,),
        in_specs=[pl.BlockSpec(memory_space=pltpu.SMEM)] + [pl.BlockSpec((K, sub, lanes), lambda i: (0, 0, i))] * 4,
        out_specs=[
            pl.BlockSpec(memory_space=pltpu.HBM),
            pl.BlockSpec((2, lanes // sub, K, sub // 2, 2 * sub), lambda i: (0, i, 0, 0, 0)),
        ],
        out_shape=[
            jax.ShapeDtypeStruct((K, sub, n * W), jnp.float32),
            jax.ShapeDtypeStruct((2, W // sub, K, sub // 2, 2 * sub), jnp.bfloat16),
        ],
        scratch_shapes=[pltpu.VMEM((2, K, sub, lanes), jnp.float32), pltpu.SemaphoreType.DMA((2,))],
        name="pairs",
    )(where, *recs)


def own_kernel(a_ref, b_ref, o_ref, tmp):
    K = a_ref.shape[0]

    def add(k, total):
        v = (a_ref[k].astype(jnp.float32) + b_ref[k].astype(jnp.float32).T) * 0.5
        tmp[k] = v
        return total + jnp.exp(v)

    norm = jnp.log(lax.fori_loop(0, K, add, jnp.zeros(tmp.shape[1:], jnp.float32), unroll=2))

    def emit(k, carry):
        o_ref[k] = (tmp[k] - norm).astype(jnp.bfloat16)
        return carry

    lax.fori_loop(0, K, emit, 0, unroll=2)


def own_pairs(tile):
    K, H, W = tile.shape
    B = 128
    return pl.pallas_call(
        own_kernel,
        grid=(H // B, W // B),
        in_specs=[pl.BlockSpec((K, B, B), lambda i, j: (0, i, j)), pl.BlockSpec((K, B, B), lambda i, j: (0, j, i))],
        out_specs=pl.BlockSpec((K, B, B), lambda i, j: (0, i, j)),
        out_shape=jax.ShapeDtypeStruct((K, H, W), jnp.bfloat16),
        scratch_shapes=[pltpu.VMEM((K, B, B), jnp.float32)],
        cost_estimate=pl.CostEstimate(flops=6 * K * H * W, bytes_accessed=6 * K * H * W, transcendentals=K * H * W),
        name="own",
    )(tile, tile)


def place_kernel(n, where_ref, mine, other, e0, e1, l0, l1, near, far, _, o_ref, own, one, two, sems):
    K, sub, W = mine.shape
    F32 = jnp.float32
    r, s, keeps = where_ref[0], where_ref[1], where_ref[KEEPS]

    def out(source, tile, q):
        spot = pl.multiple_of(lax.rem(tile, n) * W, W)
        return pltpu.make_async_copy(source, o_ref.at[:, :, pl.ds(spot, W)], sems.at[q])

    def spread(source, target):
        def body(k, carry):
            pieces = []
            for b in range(n):
                v = source[lax.rem(s + n - b, n), k].astype(jnp.float32)
                pieces.append(jnp.concatenate([v[:, :sub], v[:, sub:]], axis=0))
            target[k] = jnp.concatenate(pieces, axis=1)
            return carry

        lax.fori_loop(0, K, body, 0, unroll=4)

    def each(fn):
        def body(k, carry):
            own[k] = fn(k)
            return carry

        lax.fori_loop(0, K, body, 0, unroll=4)

    def both(a, b, k):
        return a[k].astype(F32) + b[k].astype(F32)

    beside = r + 1 - 2 * lax.rem(r, 2)

    @pl.when(s == r)
    def _():
        each(lambda k: mine[k].astype(F32))

    @pl.when(s == beside)
    def _():
        each(lambda k: other[k].astype(F32))

    @pl.when((s != r) & (s != beside) & (2 * r < n))
    def _():
        each(lambda k: jnp.concatenate([both(l0, l1, k), both(e0, e1, k)], axis=1))

    @pl.when((s != r) & (s != beside) & (2 * r >= n))
    def _():
        each(lambda k: jnp.concatenate([both(e0, e1, k), both(l0, l1, k)], axis=1))

    out(own, r, 0).start()
    spread(near, one)
    out(one, r + n - 1, 1).start()

    @pl.when(keeps == 0)
    def _():
        spread(far, two)
        out(two, r + 2, 2).start()
        out(two, r + 2, 2).wait()

    out(own, r, 0).wait()
    out(one, r + n - 1, 1).wait()


def place(where, diag, near, far, result):
    K, sub, W = diag[0].shape
    n = near.shape[0]
    vm = pl.BlockSpec(memory_space=pltpu.VMEM)
    hbm = pl.BlockSpec(memory_space=pltpu.HBM)
    return pl.pallas_call(
        functools.partial(place_kernel, n),
        in_specs=[pl.BlockSpec(memory_space=pltpu.SMEM), *[vm] * (len(diag) + 2), hbm],
        out_specs=hbm,
        out_shape=jax.ShapeDtypeStruct((K, sub, n * W), jnp.float32),
        input_output_aliases={len(diag) + 3: 0},
        scratch_shapes=[pltpu.VMEM((K, sub, W), jnp.float32)] * 3 + [pltpu.SemaphoreType.DMA((3,))],
        compiler_params=pltpu.CompilerParams(vmem_limit_bytes=40 * 1024 * 1024),
        name="place",
    )(where, *diag, near, far, result)


def plan(n):
    homes = {}
    for r in range(n):
        for c in range(n):
            gap = (c - r) % n
            if gap == 1:
                homes[r, c] = (r, 0, 0)
            elif gap == 3:
                homes[r, c] = (c, 1, 2)
            elif gap == 2:
                owner = 0 if 0 in (r, c) else 3
                homes[r, c] = (owner, int(r != owner), 1 if r == owner else 3)
    return homes


def crossing(block):
    n = lax.axis_size("rows")
    sub = block.shape[1] // (n // 2)
    got = []
    for e in range(n // 2):
        perm = [(i * n + i, i * n + (n // 2 if 2 * i < n else 0) + e) for i in range(n)]
        got.append(lax.ppermute(block[:, e * sub:(e + 1) * sub], ("rows", "cols"), perm))
    return got


def rest_kernel(h_ref, a_ref, b_ref, c_ref, near_ref, far_ref, tmp):
    K = a_ref.shape[0]
    first = pl.program_id(0) == 0

    def add(k, total):
        other = jnp.where(first, b_ref[k].astype(jnp.float32), c_ref[k].astype(jnp.float32))
        v = (a_ref[k].astype(jnp.float32) + other.T) * 0.5
        tmp[k] = v
        return total + jnp.exp(v)

    norm = jnp.log(lax.fori_loop(0, K, add, jnp.zeros(tmp.shape[1:], jnp.float32), unroll=2))

    def emit(k, carry):
        v = tmp[k] - norm
        near_ref[k] = v.astype(jnp.bfloat16)
        far_ref[k] = v.T.astype(jnp.bfloat16)
        return carry

    lax.fori_loop(0, K, emit, 0, unroll=2)


def rest_pairs(half, far_rows, near_rows):
    K, B, W = near_rows.shape
    return pl.pallas_call(
        rest_kernel,
        grid_spec=pltpu.PrefetchScalarGridSpec(
            num_scalar_prefetch=1,
            grid=(2,),
            in_specs=[
                pl.BlockSpec((K, B, B), lambda g, h: (0, 0, (1 - h[HALF]) * (1 - g) + h[HALF] * g)),
                pl.BlockSpec((K, B, B), lambda g, h: (0, 0, 1 - h[HALF])),
                pl.BlockSpec((K, B, B), lambda g, h: (0, 0, 1 - h[HALF])),
            ],
            out_specs=[
                pl.BlockSpec((K, B, B), lambda g, h: (0, 0, (1 - h[HALF]) * (1 - g) + h[HALF] * g)),
                pl.BlockSpec((K, B, B), lambda g, h: (0, 0, 0)),
            ],
            scratch_shapes=[pltpu.VMEM((K, B, B), jnp.float32)],
        ),
        out_shape=[jax.ShapeDtypeStruct((K, B, W), jnp.bfloat16), jax.ShapeDtypeStruct((K, B, B), jnp.bfloat16)],
        cost_estimate=pl.CostEstimate(flops=6 * K * B * W, bytes_accessed=6 * K * B * W, transcendentals=K * B * W),
        name="rest",
    )(half, near_rows, near_rows, far_rows)


def square(chunks, strips, recs, early, info):
    n = lax.axis_size("rows")
    axes = ("rows", "cols")
    r, s = lax.axis_index("rows"), lax.axis_index("cols")
    sub = strips[0].shape[1]
    far_rows, near_rows, *_ = lax.optimization_barrier((*chunks, *strips))
    near, far = rest_pairs(info, far_rows, near_rows)
    late = crossing(far)
    mine, other = (lax.dynamic_slice_in_dim(near, v * sub, sub, 1) for v in (r % 2, 1 - r % 2))
    other = lax.ppermute(other, axes, [(i * n + i, i * n + (i ^ 1)) for i in range(n)])
    result, msg = pairs(info, recs)
    near, far = [], []
    for k in range(n):
        t = lax.rem(s + k, n)
        for half, kept, moves in ((lax.rem(s, 2), near, [(i, (i + 1) % n) for i in range(n)]), (1 - lax.rem(s, 2), far, [(0, 2), (3, 1)])):
            payload = lax.dynamic_slice(msg, (half, t, 0, 0, 0), (1, 1) + msg.shape[2:])[0, 0]
            perm = [(i * n + j, o * n + (j + k) % n) for i, o in moves for j in range(n)]
            kept.append(lax.ppermute(payload, axes, perm))
    return place(info, [mine, other, *early, *late], jnp.stack(near), jnp.stack(far), result)[None]


def solution(mesh):
    in_specs = (P("crops", None, "rows", "cols"), P(), P(), P(), P(), P(), P())
    out_specs = P("crops", None, ("rows", "cols"), None)

    body = jax.shard_map(shards, mesh=mesh, in_specs=in_specs, out_specs=out_specs, check_vma=False)

    def run(*args):
        with jax.sharding.use_abstract_mesh(mesh.abstract_mesh):
            return body(*args)

    return run
```

```python
import functools

import jax
import jax.numpy as jnp
import numpy as np
from jax import lax
from jax.experimental.layout import Layout, with_layout_constraint
from jax.experimental import pallas as pl
from jax.experimental.pallas import tpu as pltpu
from jax.sharding import PartitionSpec as P


BLOCKS = 2
D1 = 4
D2 = 8
CHUNKS = 2

FAR = 1 << 20
ROWS = 4
LEAD = 16
KEEPS, TURN, ORDER, HALF, EDGE, PARTNER, MAIN, FIRST = 2, 3, 4, 5, 6, 10, 11, 12


def chain_kernel(cfg, info_ref, t_ref, f_ref, b_ref, e_ref, ra_ref, rb_ref, wo_ref, add_ref, o_ref, buf, side, sems, X, I, bias, acc, xa, xb, wa_ref, wb_ref):
    H, W, C, whole, chunk = cfg
    R = ROWS
    S = W + e_ref.shape[2]
    halo = BLOCKS * (D1 + D2)
    NB = R * S
    T = 256
    BF, F32 = jnp.bfloat16, jnp.float32
    start = pl.multiple_of(info_ref[FIRST + chunk], ROWS)

    def moved(source, a, b, length, q):
        return pltpu.make_async_copy(source.at[pl.ds(a, length)], buf.at[pl.ds(b, length)], sems.at[q])

    middle = moved(f_ref, start, halo, H, 0)
    middle.start()
    sides = pltpu.make_async_copy(e_ref.at[pl.ds(start, H + 2 * halo)], side, sems.at[3])
    sides.start()
    for q, edge_ref, outer, a, b in ((1, t_ref, start == 0, start - halo, 0), (2, b_ref, start + H == whole, start + H, H + halo)):

        @pl.when(outer)
        def _(q=q, edge_ref=edge_ref, b=b):
            moved(edge_ref, 0, b, halo, q).start()

        @pl.when(jnp.logical_not(outer))
        def _(q=q, a=a, b=b):
            moved(f_ref, a, b, halo, q).start()

    def at(row):
        return pl.multiple_of(128 + (row + halo + LEAD) * S, 128)

    for k in range(2 * BLOCKS):
        bias[k] = jnp.broadcast_to(add_ref[:, k:k + 1], (C, 128))

    def weights(turned):
        for raw, w in ((ra_ref, wa_ref), (rb_ref, wb_ref)):
            for k in range(BLOCKS):
                for a in range(3):
                    for b in range(3):
                        p, q = (b, a) if turned else (a, b)
                        w[k, p * C:(p + 1) * C, q * C:(q + 1) * C] = raw[k, a, :, b * C:(b + 1) * C]

    @pl.when(info_ref[TURN] > 0)
    def _():
        weights(True)

    @pl.when(info_ref[TURN] == 0)
    def _():
        weights(False)

    middle.wait()
    sides.wait()
    moved(t_ref, 0, 0, halo, 1).wait()
    moved(b_ref, 0, H + halo, halo, 2).wait()

    def fill(i, _):
        parts = []
        for q in range(R):
            e = side[i * R + q]
            parts += [e[:, :halo], buf[i * R + q], e[:, halo:]]
        X[:, pl.ds(at(i * R - halo), NB)] = jnp.concatenate(parts, axis=1)
        return 0

    lax.fori_loop(0, (H + 2 * halo) // R, fill, 0)
    lane = lax.broadcasted_iota(jnp.int32, (8, NB), 1)
    col = lane % S
    dead = ((col < halo) & (info_ref[EDGE + 2] > 0)) | ((col >= halo + W) & (info_ref[EDGE + 3] > 0))
    rl = jnp.where(dead, 4 * FAR, lane // S)
    first = jnp.where(info_ref[EDGE] > 0, -start, -FAR)
    last = jnp.where(info_ref[EDGE + 1] > 0, whole - start, FAR)

    def masked(v, row, t):
        p = rl[:, t:t + T]
        m = (p >= first - row) & (p < last - row)
        return jnp.where(m[None], v.reshape(C // 8, 8, T), 0.0).reshape(C, T)

    def biased(v, i):
        b = bias[i]
        return v + jnp.concatenate([b] * (T // 128), axis=1)

    def conv(src, d, w_ref, k, spare, emit):
        n = d // R
        ring = 2 * n + 1
        odd = H // R % 2
        lo = -spare - odd * R
        total = (H + 2 * spare) // R + odd + 2 * n

        def slot(j):
            return pl.multiple_of(lax.rem(j, ring) * NB, 128)

        def shift(j, xs):
            x = src[:, pl.ds(pl.multiple_of(at(lo - d + j * R) - 128, 128), NB + 256)]
            xs[0:C, :] = pltpu.roll(x, d, 1)[:, 128:128 + NB]
            xs[C:2 * C, :] = pltpu.roll(x, NB + 256 - d, 1)[:, 128:128 + NB]

        def step(j, xs, nxt):
            shift(j + 1, nxt)
            row = lo - d + j * R
            s0, s1, s2 = slot(j), slot(j + ring - n), slot(j + ring - 2 * n)
            for t in range(0, NB, T):
                x = jnp.concatenate([xs[0:C, t:t + T], src[:, pl.ds(at(row) + t, T)], xs[C:2 * C, t:t + T]], axis=0)
                y = jnp.dot(w_ref[k], x, preferred_element_type=F32)
                done = acc[:, pl.ds(s2 + t, T)] + y[2 * C:]
                acc[:, pl.ds(s1 + t, T)] += y[C:2 * C]
                acc[:, pl.ds(s0 + t, T)] = y[:C]
                emit(row - d, t, done)

        shift(0, xa)

        def body(i, _):
            step(2 * i, xa, xb)
            step(2 * i + 1, xb, xa)
            return 0

        lax.fori_loop(0, total // 2, body, 0)

    def block(k, carry):
        edge = (BLOCKS - k) * (D1 + D2)

        def emit_a(row, t, v):
            v = biased(v, k)
            e = jnp.where(v > 0, v, jnp.exp(v) - 1.0)
            I[:, pl.ds(at(row) + t, T)] = masked(e, row, t).astype(BF)

        conv(X, D1, wa_ref, k, edge - D1, emit_a)

        def emit_b(row, t, v):
            v = biased(v, BLOCKS + k) + X[:, pl.ds(at(row) + t, T)].astype(F32)
            X[:, pl.ds(at(row) + t, T)] = masked(v, row, t).astype(BF)

        conv(I, D2, wb_ref, k, edge - D1 - D2, emit_b)
        return carry

    lax.fori_loop(0, BLOCKS, block, 0)
    K = wo_ref.shape[0]
    bo = jnp.broadcast_to(add_ref[:K, 2 * BLOCKS:2 * BLOCKS + 1], (K, W))

    def project(i, _):
        x = X[:, pl.ds(at(i * R), NB)]
        for q in range(R):
            g = jnp.dot(wo_ref[...], x[:, q * S + halo:q * S + halo + W], preferred_element_type=F32) + bo
            o_ref[i * R + q] = g.astype(BF)
        return 0

    lax.fori_loop(0, H // R, project, 0)


def chain(info, chunk, top, field, bottom, side, wa, wb, wo, add, H):
    whole, C, W = field.shape
    S = W + side.shape[2]
    K = wo.shape[0]
    R = ROWS
    halo = BLOCKS * (D1 + D2)
    N = 128 + (H + 2 * halo + LEAD + R) * S + 256
    vm = pl.BlockSpec(memory_space=pltpu.VMEM)
    ring = (2 * (max(D1, D2) // R) + 1) * R * S
    flops = 2 * BLOCKS * 2 * 9 * C * C * H * S
    return pl.pallas_call(
        functools.partial(chain_kernel, (H, W, C, whole, chunk)),
        out_shape=jax.ShapeDtypeStruct((H, K, W), jnp.bfloat16),
        in_specs=[pl.BlockSpec(memory_space=pltpu.SMEM), *[pl.BlockSpec(memory_space=pltpu.HBM)] * 4] + [vm] * 4,
        out_specs=vm,
        scratch_shapes=[
            pltpu.VMEM((H + 2 * halo, C, W), jnp.bfloat16),
            pltpu.VMEM((H + 2 * halo, C, S - W), jnp.bfloat16),
            pltpu.SemaphoreType.DMA((4,)),
            pltpu.VMEM((C, N), jnp.bfloat16),
            pltpu.VMEM((C, N), jnp.bfloat16),
            pltpu.VMEM((2 * BLOCKS, C, 128), jnp.float32),
            pltpu.VMEM((C, ring), jnp.float32),
            pltpu.VMEM((2 * C, R * S), jnp.bfloat16),
            pltpu.VMEM((2 * C, R * S), jnp.bfloat16),
            pltpu.VMEM((BLOCKS, 3 * C, 3 * C), jnp.bfloat16),
            pltpu.VMEM((BLOCKS, 3 * C, 3 * C), jnp.bfloat16),
        ],
        compiler_params=pltpu.CompilerParams(vmem_limit_bytes=63000 * 1024),
        cost_estimate=pl.CostEstimate(flops=flops, bytes_accessed=4 * C * H * S, transcendentals=2 * C * H * S),
        name="chain",
    )(info, top, field, bottom, side, wa, wb, wo, add)


def neighbours(first, last, axis):
    peers = lax.axis_size(axis)
    up = [(i, i + 1) for i in range(peers - 1)]
    down = [(j, i) for i, j in up]
    return lax.ppermute(last, axis, up), lax.ppermute(first, axis, down)


def rims(tile):
    halo = BLOCKS * (D1 + D2)
    W = tile.shape[2]
    above, below = neighbours(tile[:, :halo], tile[:, -halo:], "rows")
    lane = jnp.arange(2 * halo)
    pick = jnp.where(lane < halo, lane, W - 2 * halo + lane)[:, None] == jnp.arange(W)[None, :]
    ends = jnp.einsum("dq,cpq->cdp", pick.astype(tile.dtype), tile, preferred_element_type=tile.dtype)
    left, right = neighbours(ends[:, :halo], ends[:, halo:], "cols")
    sides = jnp.concatenate([left, right], axis=1)
    up, down = neighbours(sides[:, :, :halo], sides[:, :, -halo:], "rows")
    corners = jnp.stack([up[:, :halo], up[:, halo:], down[:, :halo], down[:, halo:]], axis=1)
    return above, below, left, right, corners


def table(rows, cols, homes, step):
    lines = []
    for r in range(rows):
        for c in range(cols):
            diagonal = 2 * (2 * r < rows) if homes else 0
            _, turn, order = homes.get((r, c), (0, 0, diagonal))
            edge = [r == 0, r == rows - 1, c == 0, c == cols - 1]
            if turn:
                edge = edge[2:] + edge[:2]
            chunks = CHUNKS if homes else 1
            q = cols // chunks
            starts = [((j * q) ^ (order & ~(q - 1))) * step if homes else 0 for j in range(chunks)]
            apart = main = 0
            if homes:
                after = (r + 1) % rows
                first, second = homes[r, after][2], homes[after, r][2]
                apart = first ^ second
                main = (c ^ first) >> 1 if apart == 1 else (c ^ first) & 1
            lines.append([r, c, r in (0, rows - 1), turn, order, order // 2, *edge, apart == 2, main, *starts])
    return np.array(lines, np.int32)


def shards(pair_maps, conv_a, bias_a, conv_b, bias_b, out_weight, out_bias):
    rows, cols = lax.axis_size("rows"), lax.axis_size("cols")
    _, C, H, W = pair_maps.shape
    K = out_bias.shape[0]
    halo = BLOCKS * (D1 + D2)
    me = lax.axis_index("rows") * cols + lax.axis_index("cols")
    square_grid = rows == 4 and cols == 4 and H == W and H // rows == 64
    homes = plan(cols) if square_grid else {}
    lines = table(rows, cols, homes, H // cols)
    info = lax.dynamic_slice(jnp.asarray(lines), (me, 0), (1, lines.shape[1]))[0]
    add = jnp.concatenate([bias_a.T, bias_b.T, jnp.pad(out_bias, (0, C - K))[:, None]], axis=1)
    tile = pair_maps[0]
    turn, off = info[TURN], info[ORDER]

    def upright(v):
        return jnp.transpose(v, (1, 0, 2))

    field = lax.cond(turn > 0, lambda v: jnp.transpose(v, (2, 0, 1)), upright, tile) if square_grid else upright(tile)
    above, below, left, right, corners = rims(tile)
    flat = jnp.concatenate

    def sides(left, right, corners, second, third):
        west = flat([corners[:, 0], left, corners[:, third]], axis=2)
        east = flat([corners[:, second], right, corners[:, 3]], axis=2)
        return west, east

    def caller(top, bottom, west, east, length):
        gap = jnp.zeros((C, 64 - 2 * halo, west.shape[2]), west.dtype)
        west, east, top, bottom = (with_layout_constraint(v, Layout((0, 1, 2))) for v in (west, east, top, bottom))
        side = with_layout_constraint(flat([west, east, gap], axis=1), Layout((0, 1, 2)))
        side, top, bottom = lax.optimization_barrier((side, top, bottom))
        side, top, bottom = jnp.transpose(side, (2, 0, 1)), jnp.transpose(top, (1, 0, 2)), jnp.transpose(bottom, (1, 0, 2))
        return lambda info, j: chain(info, j, top, field, bottom, side, conv_a, conv_b, out_weight, add, length)

    square_grid = rows == 4 and cols == 4 and H == W and H // rows == 64

    if square_grid:
        fixed = with_layout_constraint(jnp.swapaxes(corners, 2, 3), Layout((0, 1, 2, 3)))
        corners = jnp.where(turn > 0, fixed[:, jnp.array([0, 2, 1, 3])], with_layout_constraint(corners, Layout((0, 1, 2, 3))))
        north, south, west, east = (jnp.where(turn > 0, a, b) for a, b in ((left, above), (right, below), (above, left), (below, right)))
        west, east = sides(west, east, corners, 1, 2)
        q = cols // CHUNKS
        run = caller(north, south, west, east, H // CHUNKS)
        chunks, strips, recs = [], [], []
        for j in range(CHUNKS):
            place_of = info
            if j:
                place_of, *_ = lax.optimization_barrier((info, *strips[-q:], ahead))
            chunks.append(upright(run(place_of, j)))
            for m in range(j * q, j * q + q):
                strips.append(lax.dynamic_slice_in_dim(chunks[j], ((m % q) ^ (off & (q - 1))) * (H // cols), H // cols, 1))
                perm = [(i * cols + k, home * cols + (m ^ o)) for (i, k), (home, _, o) in homes.items()]
                recs.append(lax.ppermute(strips[m], ("rows", "cols"), perm))
            if not j:
                ahead = own_pairs(lax.dynamic_slice_in_dim(chunks[0], (off & 2) * (H // cols), W // CHUNKS, 2))
                early = crossing(ahead)
        return square(chunks, strips, recs, early, info)
    west, east = sides(left, right, corners, 1, 2)
    logits = caller(above, below, west, east, H)(info, 0)
    logits = jnp.transpose(logits, (1, 0, 2))[None]
    strips = lax.all_to_all(logits, "cols", split_axis=2, concat_axis=3, tiled=True)
    flipped = lax.all_to_all(strips, ("rows", "cols"), split_axis=3, concat_axis=2, tiled=True)
    mirrored = jnp.swapaxes(flipped, 2, 3)
    symmetric = (strips.astype(jnp.float32) + mirrored.astype(jnp.float32)) * 0.5
    return symmetric - jnp.log(jnp.sum(jnp.exp(symmetric), axis=1, keepdims=True))


def pair_kernel(n, where_ref, r0, r1, r2, r3, o_ref, msg, lab, sems):
    K, sub, lanes = r0.shape
    r, keeps, main = where_ref[0], where_ref[KEEPS], where_ref[MAIN]
    apart = where_ref[PARTNER] > 0
    g = pl.program_id(0)
    W = lanes * pl.num_programs(0)

    def out(p, tile):
        spot = pl.multiple_of(lax.rem(tile, n) * W + g * lanes, lanes)
        return pltpu.make_async_copy(lab.at[p], o_ref.at[:, :, pl.ds(spot, lanes)], sems.at[p])

    for p, (one, two, far) in enumerate(((r0, r1, r2), (r3, r2, r1))):
        total = jnp.zeros((sub, lanes), jnp.float32)
        for k in range(K):
            other = jnp.where(apart, far[k].astype(jnp.float32), two[k].astype(jnp.float32))
            v = (one[k].astype(jnp.float32) + other) * 0.5
            lab[p, k] = v
            total = total + jnp.exp(v)
        norm = jnp.log(total)
        for k in range(K):
            v = lab[p, k] - norm
            lab[p, k] = v
            w = v.T
            for t in range(lanes // sub):
                b = w[t * sub:(t + 1) * sub]
                msg[p, t, k] = jnp.concatenate([b[:sub // 2], b[sub // 2:]], axis=1).astype(jnp.bfloat16)

        @pl.when(main == p)
        def _(p=p):
            out(p, r + 1).start()

        @pl.when((main != p) & (keeps > 0))
        def _(p=p):
            out(p, r + 2).start()

    for p in range(2):

        @pl.when((main == p) | (keeps > 0))
        def _(p=p):
            out(p, 0).wait()


def pairs(where, recs):
    K, sub, W = recs[0].shape
    lanes, n = 128, len(recs)
    return pl.pallas_call(
        functools.partial(pair_kernel, n),
        grid=(W // lanes,),
        in_specs=[pl.BlockSpec(memory_space=pltpu.SMEM)] + [pl.BlockSpec((K, sub, lanes), lambda i: (0, 0, i))] * 4,
        out_specs=[
            pl.BlockSpec(memory_space=pltpu.HBM),
            pl.BlockSpec((2, lanes // sub, K, sub // 2, 2 * sub), lambda i: (0, i, 0, 0, 0)),
        ],
        out_shape=[
            jax.ShapeDtypeStruct((K, sub, n * W), jnp.float32),
            jax.ShapeDtypeStruct((2, W // sub, K, sub // 2, 2 * sub), jnp.bfloat16),
        ],
        scratch_shapes=[pltpu.VMEM((2, K, sub, lanes), jnp.float32), pltpu.SemaphoreType.DMA((2,))],
        name="pairs",
    )(where, *recs)


def own_kernel(a_ref, b_ref, o_ref, tmp):
    K = a_ref.shape[0]

    def add(k, total):
        v = (a_ref[k].astype(jnp.float32) + b_ref[k].astype(jnp.float32).T) * 0.5
        tmp[k] = v
        return total + jnp.exp(v)

    norm = jnp.log(lax.fori_loop(0, K, add, jnp.zeros(tmp.shape[1:], jnp.float32), unroll=2))

    def emit(k, carry):
        o_ref[k] = (tmp[k] - norm).astype(jnp.bfloat16)
        return carry

    lax.fori_loop(0, K, emit, 0, unroll=2)


def own_pairs(tile):
    K, H, W = tile.shape
    B = 128
    return pl.pallas_call(
        own_kernel,
        grid=(H // B, W // B),
        in_specs=[pl.BlockSpec((K, B, B), lambda i, j: (0, i, j)), pl.BlockSpec((K, B, B), lambda i, j: (0, j, i))],
        out_specs=pl.BlockSpec((K, B, B), lambda i, j: (0, i, j)),
        out_shape=jax.ShapeDtypeStruct((K, H, W), jnp.bfloat16),
        scratch_shapes=[pltpu.VMEM((K, B, B), jnp.float32)],
        cost_estimate=pl.CostEstimate(flops=6 * K * H * W, bytes_accessed=6 * K * H * W, transcendentals=K * H * W),
        name="own",
    )(tile, tile)


def place_kernel(n, where_ref, mine, other, e0, e1, l0, l1, near, far, _, o_ref, own, one, two, sems):
    K, sub, W = mine.shape
    F32 = jnp.float32
    r, s, keeps = where_ref[0], where_ref[1], where_ref[KEEPS]

    def out(source, tile, q):
        spot = pl.multiple_of(lax.rem(tile, n) * W, W)
        return pltpu.make_async_copy(source, o_ref.at[:, :, pl.ds(spot, W)], sems.at[q])

    def spread(source, target):
        def body(k, carry):
            pieces = []
            for b in range(n):
                v = source[lax.rem(s + n - b, n), k].astype(jnp.float32)
                pieces.append(jnp.concatenate([v[:, :sub], v[:, sub:]], axis=0))
            target[k] = jnp.concatenate(pieces, axis=1)
            return carry

        lax.fori_loop(0, K, body, 0, unroll=4)

    def each(fn):
        def body(k, carry):
            own[k] = fn(k)
            return carry

        lax.fori_loop(0, K, body, 0, unroll=4)

    def both(a, b, k):
        return a[k].astype(F32) + b[k].astype(F32)

    beside = r + 1 - 2 * lax.rem(r, 2)

    @pl.when(s == r)
    def _():
        each(lambda k: mine[k].astype(F32))

    @pl.when(s == beside)
    def _():
        each(lambda k: other[k].astype(F32))

    @pl.when((s != r) & (s != beside) & (2 * r < n))
    def _():
        each(lambda k: jnp.concatenate([both(l0, l1, k), both(e0, e1, k)], axis=1))

    @pl.when((s != r) & (s != beside) & (2 * r >= n))
    def _():
        each(lambda k: jnp.concatenate([both(e0, e1, k), both(l0, l1, k)], axis=1))

    out(own, r, 0).start()
    spread(near, one)
    out(one, r + n - 1, 1).start()

    @pl.when(keeps == 0)
    def _():
        spread(far, two)
        out(two, r + 2, 2).start()
        out(two, r + 2, 2).wait()

    out(own, r, 0).wait()
    out(one, r + n - 1, 1).wait()


def place(where, diag, near, far, result):
    K, sub, W = diag[0].shape
    n = near.shape[0]
    vm = pl.BlockSpec(memory_space=pltpu.VMEM)
    hbm = pl.BlockSpec(memory_space=pltpu.HBM)
    return pl.pallas_call(
        functools.partial(place_kernel, n),
        in_specs=[pl.BlockSpec(memory_space=pltpu.SMEM), *[vm] * (len(diag) + 2), hbm],
        out_specs=hbm,
        out_shape=jax.ShapeDtypeStruct((K, sub, n * W), jnp.float32),
        input_output_aliases={len(diag) + 3: 0},
        scratch_shapes=[pltpu.VMEM((K, sub, W), jnp.float32)] * 3 + [pltpu.SemaphoreType.DMA((3,))],
        compiler_params=pltpu.CompilerParams(vmem_limit_bytes=40 * 1024 * 1024),
        name="place",
    )(where, *diag, near, far, result)


ORDERS = {
    (0, 1): 2, (1, 0): 3, (0, 2): 0, (2, 0): 1, (1, 2): 2, (2, 1): 3,
    (2, 3): 0, (3, 2): 1, (3, 0): 2, (0, 3): 0, (3, 1): 3, (1, 3): 1,
}


def plan(n):
    homes = {}
    for (r, c), order in ORDERS.items():
        gap = (c - r) % n
        owner = r if gap == 1 else c if gap == n - 1 else 0 if 0 in (r, c) else n - 1
        homes[r, c] = (owner, int(owner != r), order)
    return homes


def crossing(block):
    n = lax.axis_size("rows")
    sub = block.shape[1] // (n // 2)
    got = []
    for e in range(n // 2):
        perm = [(i * n + i, i * n + (n // 2 if 2 * i < n else 0) + e) for i in range(n)]
        got.append(lax.ppermute(block[:, e * sub:(e + 1) * sub], ("rows", "cols"), perm))
    return got


def rest_kernel(h_ref, a_ref, b_ref, c_ref, near_ref, far_ref, tmp):
    K = a_ref.shape[0]
    first = pl.program_id(0) == 0

    def add(k, total):
        other = jnp.where(first, b_ref[k].astype(jnp.float32), c_ref[k].astype(jnp.float32))
        v = (a_ref[k].astype(jnp.float32) + other.T) * 0.5
        tmp[k] = v
        return total + jnp.exp(v)

    norm = jnp.log(lax.fori_loop(0, K, add, jnp.zeros(tmp.shape[1:], jnp.float32), unroll=2))

    def emit(k, carry):
        v = tmp[k] - norm
        near_ref[k] = v.astype(jnp.bfloat16)
        far_ref[k] = v.T.astype(jnp.bfloat16)
        return carry

    lax.fori_loop(0, K, emit, 0, unroll=2)


def rest_pairs(half, far_rows, near_rows):
    K, B, W = near_rows.shape
    return pl.pallas_call(
        rest_kernel,
        grid_spec=pltpu.PrefetchScalarGridSpec(
            num_scalar_prefetch=1,
            grid=(2,),
            in_specs=[
                pl.BlockSpec((K, B, B), lambda g, h: (0, 0, (1 - h[HALF]) * (1 - g) + h[HALF] * g)),
                pl.BlockSpec((K, B, B), lambda g, h: (0, 0, 1 - h[HALF])),
                pl.BlockSpec((K, B, B), lambda g, h: (0, 0, 1 - h[HALF])),
            ],
            out_specs=[
                pl.BlockSpec((K, B, B), lambda g, h: (0, 0, (1 - h[HALF]) * (1 - g) + h[HALF] * g)),
                pl.BlockSpec((K, B, B), lambda g, h: (0, 0, 0)),
            ],
            scratch_shapes=[pltpu.VMEM((K, B, B), jnp.float32)],
        ),
        out_shape=[jax.ShapeDtypeStruct((K, B, W), jnp.bfloat16), jax.ShapeDtypeStruct((K, B, B), jnp.bfloat16)],
        cost_estimate=pl.CostEstimate(flops=6 * K * B * W, bytes_accessed=6 * K * B * W, transcendentals=K * B * W),
        name="rest",
    )(half, near_rows, near_rows, far_rows)


def square(chunks, strips, recs, early, info):
    n = lax.axis_size("rows")
    axes = ("rows", "cols")
    r, s = lax.axis_index("rows"), lax.axis_index("cols")
    sub = strips[0].shape[1]
    far_rows, near_rows, *_ = lax.optimization_barrier((*chunks, *strips))
    near, far = rest_pairs(info, far_rows, near_rows)
    late = crossing(far)
    mine, other = (lax.dynamic_slice_in_dim(near, v * sub, sub, 1) for v in (r % 2, 1 - r % 2))
    other = lax.ppermute(other, axes, [(i * n + i, i * n + (i ^ 1)) for i in range(n)])
    result, msg = pairs(info, recs)
    near, far = [], []
    for k in range(n):
        t = lax.rem(s + k, n)
        for half, kept, moves in ((info[MAIN], near, [(i, (i + 1) % n) for i in range(n)]), (1 - info[MAIN], far, [(0, 2), (3, 1)])):
            payload = lax.dynamic_slice(msg, (half, t, 0, 0, 0), (1, 1) + msg.shape[2:])[0, 0]
            perm = [(i * n + j, o * n + (j + k) % n) for i, o in moves for j in range(n)]
            kept.append(lax.ppermute(payload, axes, perm))
    return place(info, [mine, other, *early, *late], jnp.stack(near), jnp.stack(far), result)[None]


def solution(mesh):
    in_specs = (P("crops", None, "rows", "cols"), P(), P(), P(), P(), P(), P())
    out_specs = P("crops", None, ("rows", "cols"), None)

    body = jax.shard_map(shards, mesh=mesh, in_specs=in_specs, out_specs=out_specs, check_vma=False)

    def run(*args):
        with jax.sharding.use_abstract_mesh(mesh.abstract_mesh):
            return body(*args)

    return run
```
